512 devices in a mesh: op: 64 (over x, z, core), sec: 8 (over y).
Axes of the slice: x: 4, y: 8, z: 8, core: 2. Of those that a mesh axis runs over, the one named last changes fastest.
Arguments:
- psi: float32 [640, 8, 640], P('op', 'sec'), may hold values from -6 to 6
- left_env: float32 [64, 8, 640, 640], P('op', 'sec'), may hold values from -0.25 to 0.25
- right_env: float32 [64, 8, 640, 640], P('op', 'sec'), may hold values from -0.03125 to 0.03125
- denominators: float32 [640, 8, 640], P('op', 'sec'), may hold values from 0.5 to 4
- source_sector: int32 [64, 8], replicated, may hold values from 0 to 7
- owner: int32 [8], replicated, may hold values from 0 to 7, each once
- orders: int32 [8], replicated, may hold values from 480 to 640
Outputs:
- new_vector: float32 [640, 8, 640], P('op', 'sec')
- correction: float32 [640, 8, 640], P('op', 'sec')
The draws below stay inside these ranges and needn't reach their ends.
Inputs may be any that keep to these rules, and one draw needn't show every extreme that they name: `source_sector`: entry (t, s) is the sector from which term t maps into sector s. `owner`: each sector's slot; every slot holds one sector. Only the first orders rows and columns of a sector's block count; the inputs may hold any values beyond them, and the mask removes those entries.
All inputs are finite; a program needn't handle non-finite values.
Results may differ from the reference program's by a relative error of at most 0.0003.
Values sent between devices are 32-bit elements; how exact they have to be, the bound alone decides.
No kernel may reach another device: no remote copies, remote signals or barrier semaphores. Data moves between devices by JAX's collectives and lax.ppermute only.
A program may use at most 64 MiB of HBM per device.

```python
import math
import jax
import jax.numpy as jnp
from jax import lax

MAXO = 640
NSEC = 8
TERMS = 64


def set_ends(result, stream_key, least, largest):
    shape = result.shape
    place = [jax.random.randint(jax.random.fold_in(stream_key, axis), (), 0, shape[axis]) for axis in range(len(shape))]
    result = result.at[tuple(place)].set(least)
    longest = shape.index(max(shape))
    place[longest] = (place[longest] + 1) % shape[longest]
    return result.at[tuple(place)].set(largest)


def levels(key, extent, cuts, least, largest):
    gain = 1.0
    for position, blocks in cuts:
        draws = jax.random.uniform(jax.random.fold_in(jax.random.fold_in(key, 6), position), (blocks,), jnp.float32, least / len(cuts), largest / len(cuts))
        gain = gain * jnp.repeat(jnp.exp(draws), extent[position] // blocks).reshape((-1,) + (1,) * (len(extent) - 1 - position))
    return gain


def bell_draw(own_key, extent, deviation, reach, cuts=(), held_as=jnp.bfloat16):
    values = deviation * jax.random.normal(own_key, extent, jnp.float32)
    if cuts:
        values = values * levels(own_key, extent, cuts, -0.22, 0.18)
    return jnp.clip(values, -reach, reach).astype(held_as)


def setup_inputs(seed: int = 0) -> dict:
    key_list = jax.random.split(jax.random.key(seed), 8)
    return {
        "psi": bell_draw(key_list[0], (MAXO, NSEC, MAXO), 1.0, 6.0, ((0, 64), (1, 8)), jnp.float32),
        "left_env": bell_draw(key_list[1], (TERMS, NSEC, MAXO, MAXO), MAXO ** -0.5, 0.25, ((0, 64), (1, 8)), jnp.float32),
        "right_env": bell_draw(key_list[2], (TERMS, NSEC, MAXO, MAXO), (MAXO * TERMS) ** -0.5, 0.03125, ((0, 64), (1, 8)), jnp.float32),
        "denominators": jnp.clip(jnp.exp(math.log(4.0) - 2.0794415 * jax.random.uniform(key_list[3], (MAXO, NSEC, MAXO), jnp.float32) ** levels(key_list[3], (MAXO, NSEC, MAXO), ((0, 64), (1, 8)), -0.2, 0.2)), 0.5, 4.0),
        "source_sector": set_ends(jax.random.randint(key_list[4], (TERMS, NSEC), 0, NSEC), jax.random.fold_in(key_list[4], 1), 0, NSEC - 1).astype(jnp.int32),
        "owner": jax.random.permutation(key_list[5], NSEC).astype(jnp.int32),
        "orders": set_ends(jax.random.randint(key_list[6], (NSEC,), 3 * MAXO // 4, MAXO + 1), jax.random.fold_in(key_list[6], 1), 3 * MAXO // 4, MAXO).astype(jnp.int32),
    }


EPS = 1e-06
HIGH = lax.Precision.HIGHEST

def slot_sectors(owner):
    slots = jnp.arange(owner.shape[0], dtype=jnp.int32)
    hits = (owner[None, :] == slots[:, None]).astype(jnp.int32)
    return lax.optimization_barrier(jnp.sum(hits * slots[None, :], axis=1)).astype(jnp.int32)

def reference(psi, left_env, right_env, denominators, source_sector, owner, orders):
    sectors = slot_sectors(owner)
    order_slot = jnp.take(orders, sectors)
    line = jnp.arange(MAXO, dtype=jnp.int32)
    mask = ((line[:, None, None] < order_slot[None, :, None]) & (line[None, None, :] < order_slot[None, :, None])).astype(jnp.float32)
    source_slot = jnp.take(owner, jnp.take(source_sector, sectors, axis=1))
    count = float(MAXO * NSEC * MAXO)

    def apply(vector):

        def add_term(total, pieces):
            left, right, slots = pieces
            chosen = jnp.take(vector, slots, axis=1)
            inner = jnp.einsum('ajb,jbc->ajc', chosen, right, precision=HIGH)
            return (total + jnp.einsum('jxa,ajc->xjc', left, inner, precision=HIGH), None)
        total, _ = lax.scan(add_term, jnp.zeros_like(vector), (left_env, right_env, source_slot))
        return total * mask

    def inner_mean(first, second):
        return jnp.sum(first * second) / count
    v_raw = psi * mask
    w_raw = apply(v_raw)
    norm_raw = inner_mean(v_raw, v_raw)
    product_raw = inner_mean(v_raw, w_raw)
    scale = 1.0 / jnp.sqrt(norm_raw + EPS)
    v_zero = scale * v_raw
    w_zero = scale * w_raw
    rayleigh = product_raw / (norm_raw + EPS)
    update = (w_zero - rayleigh * v_zero) / denominators
    update_perp = update - inner_mean(v_zero, update) * v_zero
    v_one = update_perp / jnp.sqrt(inner_mean(update_perp, update_perp) + EPS)
    w_one = apply(v_one)
    corner = inner_mean(v_one, w_one)
    couple = inner_mean(v_one, w_zero)
    angle = 0.5 * jnp.arctan2(2.0 * couple, rayleigh - corner)
    sine = jnp.sin(angle)
    cosine = jnp.cos(angle)
    new_vector = sine * v_zero - cosine * v_one
    applied = sine * w_zero - cosine * w_one
    lam = sine * sine * rayleigh + cosine * cosine * corner - 2.0 * sine * cosine * couple
    correction = (applied - lam * new_vector) / denominators
    return (new_vector, correction)
```

```python
import functools

import jax
import jax.numpy as jnp
from jax import lax
from jax.experimental import pallas as pl
from jax.experimental.pallas import tpu as pltpu
from jax.sharding import Mesh
from jax.sharding import PartitionSpec as P

CHIP = ("op_0", "op_1")
OP = ("op_0", "op_1", "op_2")
EPS = 1e-06
LANES = 128
VMEM = pl.BlockSpec(memory_space=pltpu.VMEM)
SMEM = pl.BlockSpec(memory_space=pltpu.SMEM)


def up8(n):
    return -(-n // 8) * 8


def op_position():
    sizes = [lax.axis_size(a) for a in OP]
    return (lax.axis_index("op_0") * sizes[1] + lax.axis_index("op_1")) * sizes[2] + lax.axis_index("op_2")


def sector_at(owner_ref, slot, nsec):
    found = jnp.int32(0)
    for s in range(nsec):
        found = found + jnp.where(owner_ref[s] == slot, s, 0)
    return found


def row_mask(order, lines, per_row, first_row):
    line = lax.broadcasted_iota(jnp.int32, (lines, LANES), 0)
    lane = lax.broadcasted_iota(jnp.int32, (lines, LANES), 1)
    row = line // per_row
    col = (line - row * per_row) * LANES + lane
    return (first_row + row < order) & (col < order)


def total(x):
    return jnp.sum(jnp.sum(x, axis=0, keepdims=True), axis=1, keepdims=True)


def lane_row(values):
    lane = lax.broadcasted_iota(jnp.int32, (1, LANES), 1)
    out = jnp.zeros((1, LANES), jnp.float32)
    for i, v in enumerate(values):
        out = jnp.where(lane == i, v, out)
    return out


def prep_kernel(per_row, nsec, pad, owner_ref, orders_ref, psi_ref, den_ref, v_ref, out_ref):
    lines = psi_ref.shape[0]
    rows = lines // per_row
    order = orders_ref[sector_at(owner_ref, lax.axis_index("sec"), nsec)]
    keep = row_mask(order, lines, per_row, op_position() * rows)
    v = jnp.where(keep, psi_ref[...], 0.0)
    d = den_ref[...]
    v_ref[...] = v
    for y in range(nsec):
        out_ref[2 * y * pad : 2 * y * pad + lines, :] = v
        out_ref[(2 * y + 1) * pad : (2 * y + 1) * pad + lines, :] = d
        if pad > lines:
            out_ref[2 * y * pad + lines : (2 * y + 1) * pad, :] = jnp.zeros((pad - lines, LANES), jnp.float32)
            out_ref[(2 * y + 1) * pad + lines : (2 * y + 2) * pad, :] = jnp.ones((pad - lines, LANES), jnp.float32)


def spread(table_ref, owner_ref, source_ref, out_ref, lines, pitch, nsec):
    sector = sector_at(owner_ref, lax.axis_index("sec"), nsec)
    for t in range(out_ref.shape[0] // lines):
        slot = owner_ref[source_ref[sector, t]]
        start = pl.multiple_of(slot * pitch, 8)
        out_ref[t * lines : (t + 1) * lines, :] = table_ref[pl.ds(start, lines), :]


def select_kernel(lines, pad, nsec, owner_ref, source_ref, vd_ref, out_ref):
    spread(vd_ref, owner_ref, source_ref, out_ref, lines, 2 * pad, nsec)


def halves(x):
    hi = x.astype(jnp.bfloat16)
    return hi, (x - hi.astype(jnp.float32)).astype(jnp.bfloat16)


def dot3(a_hi, a_lo, b_hi, b_lo):
    dot = functools.partial(jnp.dot, preferred_element_type=jnp.float32)
    return dot(a_hi, b_hi) + (dot(a_hi, b_lo) + dot(a_lo, b_hi))


def split_kernel(rows, left_ref, right_ref, lh_ref, ll_ref, rh_ref, rl_ref, order_ref):
    width = left_ref.shape[0]
    half = width // 2
    mine = lax.axis_index("op_2") == 0
    for q in range(width // (2 * rows)):
        a = left_ref[2 * q * rows : (2 * q + 1) * rows, :]
        b = left_ref[(2 * q + 1) * rows : (2 * q + 2) * rows, :]
        order_ref[q * rows : (q + 1) * rows, :] = jnp.where(mine, b, a)
        order_ref[half + q * rows : half + (q + 1) * rows, :] = jnp.where(mine, a, b)
    step = 160

    def body(m, carry):
        at = pl.ds(pl.multiple_of(m * step, step), step)
        lh_ref[at, :], ll_ref[at, :] = halves(order_ref[at, :])
        rh_ref[at, :], rl_ref[at, :] = halves(right_ref[at, :])
        return carry

    lax.fori_loop(0, width // step, body, 0)


def left_product(lh_ref, ll_ref, ih_ref, il_ref, out_ref, first, per_row):
    step = 160
    for m in range(out_ref.shape[0] // per_row // step):
        at = pl.ds(first + m * step, step)
        y = dot3(lh_ref[at, :], ll_ref[at, :], ih_ref[...], il_ref[...])
        for k in range(per_row):
            out_ref[pl.ds(m * step * per_row + k, step, stride=per_row), :] = y[:, k * LANES : (k + 1) * LANES]


def inner_kernel(per_row, x_ref, rh_ref, rl_ref, lh_ref, ll_ref, ih_ref, il_ref, out_ref):
    width = rh_ref.shape[0]
    step = 160
    for m in range(width // step):
        x = jnp.concatenate(
            [x_ref[pl.ds(m * step * per_row + k, step, stride=per_row), :] for k in range(per_row)], axis=1
        )
        x_hi, x_lo = halves(x)
        at = pl.ds(m * step, step)
        ih_ref[at, :], il_ref[at, :] = halves(dot3(x_hi, x_lo, rh_ref[...], rl_ref[...]))
    left_product(lh_ref, ll_ref, ih_ref, il_ref, out_ref, 0, per_row)


def own_kernel(per_row, lh_ref, ll_ref, ih_ref, il_ref, out_ref):
    left_product(lh_ref, ll_ref, ih_ref, il_ref, out_ref, lh_ref.shape[0] // 2, per_row)


def masked_sum(part_ref, owner_ref, orders_ref, lines, per_row, nsec):
    parts = part_ref.shape[0] // lines
    w = part_ref[0:lines, :]
    for q in range(1, parts):
        w = w + part_ref[q * lines : (q + 1) * lines, :]
    order = orders_ref[sector_at(owner_ref, lax.axis_index("sec"), nsec)]
    keep = row_mask(order, lines, per_row, op_position() * (lines // per_row))
    return jnp.where(keep, w, 0.0)


def share_kernel(lines, pad, per_row, nsec, owner_ref, orders_ref, part_ref, w_ref, out_ref):
    w = masked_sum(part_ref, owner_ref, orders_ref, lines, per_row, nsec)
    w_ref[...] = w
    for y in range(nsec):
        out_ref[y * pad : y * pad + lines, :] = w
        if pad > lines:
            out_ref[y * pad + lines : (y + 1) * pad, :] = jnp.zeros((pad - lines, LANES), jnp.float32)


def first_sums_kernel(pad, nsec, vd_ref, w8_ref, out_ref):
    vv = jnp.zeros((pad, LANES), jnp.float32)
    vw = jnp.zeros((pad, LANES), jnp.float32)
    for y in range(nsec):
        v = vd_ref[2 * y * pad : (2 * y + 1) * pad, :]
        vv = vv + v * v
        vw = vw + v * w8_ref[y * pad : (y + 1) * pad, :]
    out_ref[...] = jnp.broadcast_to(lane_row([total(vv), total(vw)]), out_ref.shape)


def update_kernel(lines, pad, nsec, count, owner_ref, source_ref, sums_ref, vd_ref, w8_ref, out_ref, t_ref, scal_ref, t8_ref):
    sums = jnp.sum(sums_ref[...], axis=0, keepdims=True) / count
    norm, product = sums[:, 0:1], sums[:, 1:2]
    scale = 1.0 / jnp.sqrt(norm + EPS)
    rayleigh = product / (norm + EPS)
    for y in range(nsec):
        v0 = scale * vd_ref[2 * y * pad : (2 * y + 1) * pad, :]
        d = vd_ref[(2 * y + 1) * pad : (2 * y + 2) * pad, :]
        w0 = scale * w8_ref[y * pad : (y + 1) * pad, :]
        t8_ref[y * pad : (y + 1) * pad, :] = (w0 - rayleigh * v0) / d
    t_ref[...] = t8_ref[pl.ds(pl.multiple_of(lax.axis_index("sec") * pad, 8), lines), :]
    scal_ref[...] = jnp.broadcast_to(lane_row([norm, product]), scal_ref.shape)
    spread(t8_ref, owner_ref, source_ref, out_ref, lines, pad, nsec)


def last_sums_kernel(lines, per_row, nsec, owner_ref, orders_ref, part_ref, scal_ref, v_ref, w_ref, t_ref, h_ref, out_ref):
    h = masked_sum(part_ref, owner_ref, orders_ref, lines, per_row, nsec)
    h_ref[...] = h
    scale = 1.0 / jnp.sqrt(scal_ref[0:1, 0:1] + EPS)
    v0 = scale * v_ref[...]
    w0 = scale * w_ref[...]
    t = t_ref[...]
    sums = [total(v0 * t), total(t * t), total(t * w0), total(t * h), total(v0 * h)]
    out_ref[...] = jnp.broadcast_to(lane_row(sums), out_ref.shape)


def relay_kernel(in_ref, out_ref):
    out_ref[...] = jnp.broadcast_to(jnp.sum(in_ref[...], axis=0, keepdims=True), out_ref.shape)


def final_kernel(count, sums_ref, scal_ref, v_ref, w_ref, t_ref, h_ref, den_ref, new_ref, corr_ref):
    norm, product = scal_ref[0:1, 0:1], scal_ref[0:1, 1:2]
    sums = jnp.sum(sums_ref[...], axis=0, keepdims=True) / count
    along, tt, tw, th, vh = (sums[:, i : i + 1] for i in range(5))
    scale = 1.0 / jnp.sqrt(norm + EPS)
    rayleigh = product / (norm + EPS)
    vv = norm / (norm + EPS)
    tail = tt - 2.0 * along * along + along * along * vv
    inv = 1.0 / jnp.sqrt(tail + EPS)
    corner = inv * inv * (th - along * (tw + vh) + along * along * rayleigh)
    couple = inv * (tw - along * rayleigh)
    y = 2.0 * couple
    x = rayleigh - corner
    big = jnp.maximum(jnp.abs(x), jnp.abs(y))
    none = big == 0.0
    big = jnp.where(none, 1.0, big)
    xs = jnp.where(none, 1.0, x / big)
    ys = y / big
    hyp = jnp.sqrt(xs * xs + ys * ys)
    major = jnp.sqrt((hyp + jnp.abs(xs)) / (2.0 * hyp))
    minor = jnp.abs(ys) / (2.0 * hyp * major)
    ahead = xs > 0.0
    cosine = jnp.where(ahead, major, minor)
    sine = jnp.where(ys < 0.0, -1.0, 1.0) * jnp.where(ahead, minor, major)
    v0 = scale * v_ref[...]
    w0 = scale * w_ref[...]
    v1 = inv * (t_ref[...] - along * v0)
    w1 = inv * (h_ref[...] - along * w0)
    new = sine * v0 - cosine * v1
    applied = sine * w0 - cosine * w1
    lam = sine * sine * rayleigh + cosine * cosine * corner - 2.0 * sine * cosine * couple
    new_ref[...] = new
    corr_ref[...] = (applied - lam * new) / den_ref[...]


def f32(*shape):
    return jax.ShapeDtypeStruct(shape, jnp.float32)


def bf16(*shape):
    return jax.ShapeDtypeStruct(shape, jnp.bfloat16)


def call(kernel, out, smem, vmem, scratch=()):
    return pl.pallas_call(
        kernel,
        out_shape=out,
        in_specs=[SMEM] * len(smem) + [VMEM] * len(vmem),
        out_specs=jax.tree.map(lambda _: VMEM, out),
        scratch_shapes=scratch,
        compiler_params=pltpu.CompilerParams(vmem_limit_bytes=32 * 1024 * 1024),
    )(*smem, *vmem)


def exchange(x, axis, parts):
    lines = x.shape[0] // parts
    y = lax.all_to_all(x.reshape(parts, lines, 1, LANES), axis, 0, 0, tiled=True)
    return y.reshape(x.shape)


def per_device(psi, left_env, right_env, denominators, source_sector, owner, orders):
    rows = psi.shape[0]
    width = psi.shape[2]
    per_row = width // LANES
    lines = rows * per_row
    pad = up8(lines)
    nop = lax.axis_size(OP)
    nchip = lax.axis_size(CHIP)
    nsec = lax.axis_size("sec")
    count = float(width * nsec * width)
    left = left_env.reshape(width, width)
    right = right_env.reshape(width, width)
    source = source_sector.T
    psi_l = psi.reshape(lines, LANES)
    den_l = denominators.reshape(lines, LANES)
    part = functools.partial
    swap = [(0, 1), (1, 0)]

    v, vd = call(
        part(prep_kernel, per_row, nsec, pad),
        (f32(lines, LANES), f32(2 * nsec * pad, LANES)),
        (owner, orders),
        (psi_l, den_l),
    )
    vd8 = exchange(vd, "sec", nsec)
    lh, ll, rh, rl = call(
        part(split_kernel, rows),
        (bf16(width, width),) * 4,
        (),
        (left, right),
        scratch=[pltpu.VMEM((width, width), jnp.float32)],
    )

    def products(x):
        ih, il, other = call(
            part(inner_kernel, per_row),
            (bf16(width, width), bf16(width, width), f32(width * per_row // 2, LANES)),
            (),
            (x, rh, rl, lh, ll),
        )
        came = lax.ppermute(other, "op_2", swap)
        own = call(part(own_kernel, per_row), f32(width * per_row // 2, LANES), (), (lh, ll, ih, il))
        return exchange(own + came, CHIP, nchip)

    chosen = call(part(select_kernel, lines, pad, nsec), f32(nop * lines, LANES), (owner, source), (vd8,))
    parts = products(exchange(chosen, OP, nop))
    w, w_out = call(
        part(share_kernel, lines, pad, per_row, nsec),
        (f32(lines, LANES), f32(nsec * pad, LANES)),
        (owner, orders),
        (parts,),
    )
    w8 = exchange(w_out, "sec", nsec)
    sums = call(part(first_sums_kernel, pad, nsec), f32(nop, LANES), (), (vd8, w8))
    sums = exchange(sums, OP, nop)
    chosen, t, scal = call(
        part(update_kernel, lines, pad, nsec, count),
        (f32(nop * lines, LANES), f32(lines, LANES), f32(8, LANES)),
        (owner, source),
        (sums, vd8, w8),
        scratch=[pltpu.VMEM((nsec * pad, LANES), jnp.float32)],
    )
    parts = products(exchange(chosen, OP, nop))
    h, sums = call(
        part(last_sums_kernel, lines, per_row, nsec),
        (f32(lines, LANES), f32(nsec, LANES)),
        (owner, orders),
        (parts, scal, v, w, t),
    )
    sums = exchange(sums, "sec", nsec)
    sums = call(relay_kernel, f32(nop, LANES), (), (sums,))
    sums = exchange(sums, OP, nop)
    new, corr = call(
        part(final_kernel, count),
        (f32(lines, LANES), f32(lines, LANES)),
        (),
        (sums, scal, v, w, t, h, den_l),
    )
    return new.reshape(psi.shape), corr.reshape(psi.shape)


def solution(mesh):
    sec = mesh.shape["sec"]
    torus = Mesh(mesh.devices.reshape(4, 8, 2, sec), (*OP, "sec"))
    specs = (
        P(OP, "sec", None),
        P(OP, "sec", None, None),
        P(OP, "sec", None, None),
        P(OP, "sec", None),
        P(),
        P(),
        P(),
    )
    outs = (P(OP, "sec", None), P(OP, "sec", None))
    return jax.shard_map(per_device, mesh=torus, in_specs=specs, out_specs=outs, check_vma=False)
```

```python
import functools

import jax
import jax.numpy as jnp
from jax import lax
from jax.experimental import pallas as pl
from jax.experimental.pallas import tpu as pltpu
from jax.sharding import Mesh
from jax.sharding import PartitionSpec as P

CHIP = ("op_0", "op_1")
OP = ("op_0", "op_1", "op_2")
EPS = 1e-06
LANES = 128
VMEM = pl.BlockSpec(memory_space=pltpu.VMEM)
SMEM = pl.BlockSpec(memory_space=pltpu.SMEM)


def up8(n):
    return -(-n // 8) * 8


def op_position():
    sizes = [lax.axis_size(a) for a in OP]
    return (lax.axis_index("op_0") * sizes[1] + lax.axis_index("op_1")) * sizes[2] + lax.axis_index("op_2")


def sector_at(owner_ref, slot, nsec):
    found = jnp.int32(0)
    for s in range(nsec):
        found = found + jnp.where(owner_ref[s] == slot, s, 0)
    return found


def row_mask(order, lines, per_row, first_row):
    line = lax.broadcasted_iota(jnp.int32, (lines, LANES), 0)
    lane = lax.broadcasted_iota(jnp.int32, (lines, LANES), 1)
    row = line // per_row
    col = (line - row * per_row) * LANES + lane
    return (first_row + row < order) & (col < order)


def total(x):
    return jnp.sum(jnp.sum(x, axis=0, keepdims=True), axis=1, keepdims=True)


def lane_row(values):
    lane = lax.broadcasted_iota(jnp.int32, (1, LANES), 1)
    out = jnp.zeros((1, LANES), jnp.float32)
    for i, v in enumerate(values):
        out = jnp.where(lane == i, v, out)
    return out


def prep_kernel(per_row, nsec, pad, owner_ref, orders_ref, psi_ref, den_ref, v_ref, v_out_ref, d_out_ref):
    rows, width = psi_ref.shape[0], psi_ref.shape[2]
    lines = rows * per_row
    order = orders_ref[sector_at(owner_ref, lax.axis_index("sec"), nsec)]
    row = lax.broadcasted_iota(jnp.int32, (rows, width), 0) + op_position() * rows
    col = lax.broadcasted_iota(jnp.int32, (rows, width), 1)
    v = jnp.where((row < order) & (col < order), psi_ref[:, 0, :], 0.0)
    d = den_ref[:, 0, :]
    for k in range(per_row):
        part = slice(k * LANES, (k + 1) * LANES)
        at = pl.ds(k, rows, stride=per_row)
        v_ref[at, :] = v[:, part]
        d_out_ref[at, :] = d[:, part]
        for y in range(nsec):
            at = pl.ds(y * pad + k, rows, stride=per_row)
            v_out_ref[at, :] = v[:, part]
    if pad > lines:
        for y in range(nsec):
            v_out_ref[y * pad + lines : (y + 1) * pad, :] = jnp.zeros((pad - lines, LANES), jnp.float32)
        d_out_ref[lines:pad, :] = jnp.ones((pad - lines, LANES), jnp.float32)


def spread(table_ref, owner_ref, source_ref, out_ref, lines, pitch, nsec):
    sector = sector_at(owner_ref, lax.axis_index("sec"), nsec)
    for t in range(out_ref.shape[0] // lines):
        slot = owner_ref[source_ref[sector, t]]
        start = pl.multiple_of(slot * pitch, 8)
        out_ref[t * lines : (t + 1) * lines, :] = table_ref[pl.ds(start, lines), :]


def select_kernel(lines, pad, nsec, owner_ref, source_ref, v8_ref, d_ref, out_ref, d_out_ref):
    d_out_ref[...] = d_ref[...]
    spread(v8_ref, owner_ref, source_ref, out_ref, lines, pad, nsec)


def halves(x):
    hi = x.astype(jnp.bfloat16)
    return hi, (x - hi.astype(jnp.float32)).astype(jnp.bfloat16)


def dot3(a_hi, a_lo, b_hi, b_lo):
    dot = functools.partial(jnp.dot, preferred_element_type=jnp.float32)
    return dot(a_hi, b_hi) + (dot(a_hi, b_lo) + dot(a_lo, b_hi))


def split_rows(x_ref, hi_ref, lo_ref):
    step = 160

    def body(m, carry):
        at = pl.ds(pl.multiple_of(m * step, step), step)
        hi_ref[at, :], lo_ref[at, :] = halves(x_ref[at, :])
        return carry

    lax.fori_loop(0, x_ref.shape[0] // step, body, 0)


def split_kernel(rows, left_ref, right_ref, mats_ref, order_ref):
    width = left_ref.shape[0]
    half = width // 2
    mine = lax.axis_index("op_2") == 0
    for q in range(width // (2 * rows)):
        a = left_ref[2 * q * rows : (2 * q + 1) * rows, :]
        b = left_ref[(2 * q + 1) * rows : (2 * q + 2) * rows, :]
        order_ref[q * rows : (q + 1) * rows, :] = jnp.where(mine, b, a)
        order_ref[half + q * rows : half + (q + 1) * rows, :] = jnp.where(mine, a, b)
    split_rows(order_ref, mats_ref.at[0], mats_ref.at[1])
    split_rows(right_ref, mats_ref.at[2], mats_ref.at[3])


def left_product(mats_ref, ih_ref, il_ref, out_ref, first, per_row):
    step = 160
    for m in range(out_ref.shape[0] // per_row // step):
        at = pl.ds(first + m * step, step)
        y = dot3(mats_ref[0, at, :], mats_ref[1, at, :], ih_ref[...], il_ref[...])
        for k in range(per_row):
            out_ref[pl.ds(m * step * per_row + k, step, stride=per_row), :] = y[:, k * LANES : (k + 1) * LANES]


def inner_kernel(per_row, x_ref, mats_ref, ih_ref, il_ref, out_ref):
    width = mats_ref.shape[1]
    step = 160
    for m in range(width // step):
        x = jnp.concatenate(
            [x_ref[pl.ds(m * step * per_row + k, step, stride=per_row), :] for k in range(per_row)], axis=1
        )
        x_hi, x_lo = halves(x)
        at = pl.ds(m * step, step)
        ih_ref[at, :], il_ref[at, :] = halves(dot3(x_hi, x_lo, mats_ref[2], mats_ref[3]))
    left_product(mats_ref, ih_ref, il_ref, out_ref, 0, per_row)


def own_kernel(per_row, mats_ref, ih_ref, il_ref, out_ref):
    left_product(mats_ref, ih_ref, il_ref, out_ref, mats_ref.shape[1] // 2, per_row)


def masked_sum(part_ref, owner_ref, orders_ref, lines, per_row, nsec):
    parts = part_ref.shape[0] // lines
    w = part_ref[0:lines, :]
    for q in range(1, parts):
        w = w + part_ref[q * lines : (q + 1) * lines, :]
    order = orders_ref[sector_at(owner_ref, lax.axis_index("sec"), nsec)]
    keep = row_mask(order, lines, per_row, op_position() * (lines // per_row))
    return jnp.where(keep, w, 0.0)


def share_kernel(lines, pad, per_row, nsec, owner_ref, orders_ref, part_ref, w_ref, out_ref):
    w = masked_sum(part_ref, owner_ref, orders_ref, lines, per_row, nsec)
    w_ref[...] = w
    for y in range(nsec):
        out_ref[y * pad : y * pad + lines, :] = w
        if pad > lines:
            out_ref[y * pad + lines : (y + 1) * pad, :] = jnp.zeros((pad - lines, LANES), jnp.float32)


def first_sums_kernel(pad, nsec, v8_ref, w8_ref, out_ref):
    vv = jnp.zeros((pad, LANES), jnp.float32)
    vw = jnp.zeros((pad, LANES), jnp.float32)
    for y in range(nsec):
        v = v8_ref[y * pad : (y + 1) * pad, :]
        vv = vv + v * v
        vw = vw + v * w8_ref[y * pad : (y + 1) * pad, :]
    out_ref[...] = jnp.broadcast_to(lane_row([total(vv), total(vw)]), out_ref.shape)


def update_kernel(lines, pad, nsec, count, owner_ref, source_ref, sums_ref, v8_ref, d8_ref, w8_ref, out_ref, t_ref, scal_ref, t8_ref):
    sums = jnp.sum(sums_ref[...], axis=0, keepdims=True) / count
    norm, product = sums[:, 0:1], sums[:, 1:2]
    scale = 1.0 / jnp.sqrt(norm + EPS)
    rayleigh = product / (norm + EPS)
    me = lax.axis_index("sec")
    for k in range(nsec):
        slot = lax.rem(me + nsec - k, nsec)
        at = pl.ds(pl.multiple_of(slot * pad, 8), pad)
        t8_ref[at, :] = (scale * w8_ref[at, :] - rayleigh * (scale * v8_ref[at, :])) / d8_ref[k * pad : (k + 1) * pad, :]
    t_ref[...] = t8_ref[pl.ds(pl.multiple_of(me * pad, 8), lines), :]
    scal_ref[...] = jnp.broadcast_to(lane_row([norm, product]), scal_ref.shape)
    spread(t8_ref, owner_ref, source_ref, out_ref, lines, pad, nsec)


def last_sums_kernel(lines, per_row, nsec, owner_ref, orders_ref, part_ref, scal_ref, v_ref, w_ref, t_ref, h_ref, out_ref):
    h = masked_sum(part_ref, owner_ref, orders_ref, lines, per_row, nsec)
    h_ref[...] = h
    scale = 1.0 / jnp.sqrt(scal_ref[0:1, 0:1] + EPS)
    v0 = scale * v_ref[...]
    w0 = scale * w_ref[...]
    t = t_ref[...]
    sums = [total(v0 * t), total(t * t), total(t * w0), total(t * h), total(v0 * h)]
    out_ref[...] = jnp.broadcast_to(lane_row(sums), out_ref.shape)


def final_kernel(count, per_row, sums_ref, scal_ref, v_ref, w_ref, t_ref, h_ref, d_ref, new_ref, corr_ref, new_lines, corr_lines):
    norm, product = scal_ref[0:1, 0:1], scal_ref[0:1, 1:2]
    sums = jnp.sum(sums_ref[...], axis=0, keepdims=True) / count
    along, tt, tw, th, vh = (sums[:, i : i + 1] for i in range(5))
    scale = 1.0 / jnp.sqrt(norm + EPS)
    rayleigh = product / (norm + EPS)
    vv = norm / (norm + EPS)
    tail = tt - 2.0 * along * along + along * along * vv
    inv = 1.0 / jnp.sqrt(tail + EPS)
    corner = inv * inv * (th - along * (tw + vh) + along * along * rayleigh)
    couple = inv * (tw - along * rayleigh)
    y = 2.0 * couple
    x = rayleigh - corner
    big = jnp.maximum(jnp.abs(x), jnp.abs(y))
    none = big == 0.0
    big = jnp.where(none, 1.0, big)
    xs = jnp.where(none, 1.0, x / big)
    ys = y / big
    hyp = jnp.sqrt(xs * xs + ys * ys)
    major = jnp.sqrt((hyp + jnp.abs(xs)) / (2.0 * hyp))
    minor = jnp.abs(ys) / (2.0 * hyp * major)
    ahead = xs > 0.0
    cosine = jnp.where(ahead, major, minor)
    sine = jnp.where(ys < 0.0, -1.0, 1.0) * jnp.where(ahead, minor, major)
    v0 = scale * v_ref[...]
    w0 = scale * w_ref[...]
    v1 = inv * (t_ref[...] - along * v0)
    w1 = inv * (h_ref[...] - along * w0)
    new = sine * v0 - cosine * v1
    applied = sine * w0 - cosine * w1
    lam = sine * sine * rayleigh + cosine * cosine * corner - 2.0 * sine * cosine * couple
    new_lines[...] = new
    corr_lines[...] = (applied - lam * new) / d_ref[0 : new.shape[0], :]
    rows = new_ref.shape[0]
    for k in range(per_row):
        at, part = pl.ds(k, rows, stride=per_row), slice(k * LANES, (k + 1) * LANES)
        new_ref[:, 0, part] = new_lines[at, :]
        corr_ref[:, 0, part] = corr_lines[at, :]


def f32(*shape):
    return jax.ShapeDtypeStruct(shape, jnp.float32)


def bf16(*shape):
    return jax.ShapeDtypeStruct(shape, jnp.bfloat16)


def call(kernel, out, smem, vmem, scratch=()):
    return pl.pallas_call(
        kernel,
        out_shape=out,
        in_specs=[SMEM] * len(smem) + [VMEM] * len(vmem),
        out_specs=jax.tree.map(lambda _: VMEM, out),
        scratch_shapes=scratch,
        compiler_params=pltpu.CompilerParams(vmem_limit_bytes=32 * 1024 * 1024),
    )(*smem, *vmem)


def exchange(x, axis, parts):
    lines = x.shape[0] // parts
    y = lax.all_to_all(x.reshape(parts, lines, 1, LANES), axis, 0, 0, tiled=True)
    return y.reshape(x.shape)


def per_device(psi, left_env, right_env, denominators, source_sector, owner, orders):
    rows = psi.shape[0]
    width = psi.shape[2]
    per_row = width // LANES
    lines = rows * per_row
    pad = up8(lines)
    nop = lax.axis_size(OP)
    nchip = lax.axis_size(CHIP)
    nsec = lax.axis_size("sec")
    count = float(width * nsec * width)
    left = left_env.reshape(width, width)
    right = right_env.reshape(width, width)
    source = source_sector.T
    part = functools.partial
    swap = [(0, 1), (1, 0)]

    v, v_out, d_out = call(
        part(prep_kernel, per_row, nsec, pad),
        (f32(lines, LANES), f32(nsec * pad, LANES), f32(pad, LANES)),
        (owner, orders),
        (psi, denominators),
    )
    v8 = exchange(v_out, "sec", nsec)
    square = bf16(width, width)
    half = f32(width * per_row // 2, LANES)
    mats = call(
        part(split_kernel, rows),
        bf16(4, width, width),
        (),
        (left, right),
        scratch=[pltpu.VMEM((width, width), jnp.float32)],
    )

    def products(x):
        ih, il, other = call(part(inner_kernel, per_row), (square, square, half), (), (x, mats))
        came = lax.ppermute(other, "op_2", swap)
        own = call(part(own_kernel, per_row), half, (), (mats, ih, il))
        return exchange(own + came, CHIP, nchip)

    chosen, d8 = call(
        part(select_kernel, lines, pad, nsec),
        (f32(nop * lines, LANES), f32(pad, LANES)),
        (owner, source),
        (v8, d_out),
    )
    chosen = exchange(chosen, OP, nop)
    reach = 1
    while reach < nsec:
        came = lax.ppermute(d8, "sec", [(i, (i + reach) % nsec) for i in range(nsec)])
        d8 = jnp.concatenate([d8, came], axis=0)
        reach *= 2
    chosen, d8 = lax.optimization_barrier((chosen, d8))
    parts = products(chosen)
    w, w_out = call(
        part(share_kernel, lines, pad, per_row, nsec),
        (f32(lines, LANES), f32(nsec * pad, LANES)),
        (owner, orders),
        (parts,),
    )
    w8 = exchange(w_out, "sec", nsec)
    sums = call(part(first_sums_kernel, pad, nsec), f32(nop, LANES), (), (v8, w8))
    sums = exchange(sums, OP, nop)
    chosen, t, scal = call(
        part(update_kernel, lines, pad, nsec, count),
        (f32(nop * lines, LANES), f32(lines, LANES), f32(8, LANES)),
        (owner, source),
        (sums, v8, d8, w8),
        scratch=[pltpu.VMEM((nsec * pad, LANES), jnp.float32)],
    )
    parts = products(exchange(chosen, OP, nop))
    h, sums = call(
        part(last_sums_kernel, lines, per_row, nsec),
        (f32(lines, LANES), f32(1, LANES)),
        (owner, orders),
        (parts, scal, v, w, t),
    )
    chips = nchip * nsec
    sums = jnp.broadcast_to(lax.psum(sums, "op_2"), (chips, LANES))
    sums = exchange(sums, (*CHIP, "sec"), chips)
    return call(
        part(final_kernel, count, per_row),
        (f32(*psi.shape), f32(*psi.shape)),
        (),
        (sums, scal, v, w, t, h, d_out),
        scratch=[pltpu.VMEM((lines, LANES), jnp.float32)] * 2,
    )


def solution(mesh):
    sec = mesh.shape["sec"]
    torus = Mesh(mesh.devices.reshape(4, 8, 2, sec), (*OP, "sec"))
    specs = (
        P(OP, "sec", None),
        P(OP, "sec", None, None),
        P(OP, "sec", None, None),
        P(OP, "sec", None),
        P(),
        P(),
        P(),
    )
    outs = (P(OP, "sec", None), P(OP, "sec", None))
    return jax.shard_map(per_device, mesh=torus, in_specs=specs, out_specs=outs, check_vma=False)
```

```python
import functools

import jax
import jax.numpy as jnp
from jax import lax
from jax.experimental import pallas as pl
from jax.experimental.pallas import tpu as pltpu
from jax.sharding import Mesh
from jax.sharding import PartitionSpec as P

CHIP = ("op_0", "op_1")
OP = ("op_0", "op_1", "op_2")
EPS = 1e-06
LANES = 128
VMEM = pl.BlockSpec(memory_space=pltpu.VMEM)
SMEM = pl.BlockSpec(memory_space=pltpu.SMEM)
ANY = pl.BlockSpec(memory_space=pl.ANY)


def up8(n):
    return -(-n // 8) * 8


def op_position():
    sizes = [lax.axis_size(a) for a in OP]
    return (lax.axis_index("op_0") * sizes[1] + lax.axis_index("op_1")) * sizes[2] + lax.axis_index("op_2")


def sector_at(owner_ref, slot, nsec):
    found = jnp.int32(0)
    for s in range(nsec):
        found = found + jnp.where(owner_ref[s] == slot, s, 0)
    return found


def row_mask(order, lines, per_row, first_row):
    line = lax.broadcasted_iota(jnp.int32, (lines, LANES), 0)
    lane = lax.broadcasted_iota(jnp.int32, (lines, LANES), 1)
    row = line // per_row
    col = (line - row * per_row) * LANES + lane
    return (first_row + row < order) & (col < order)


def total(x):
    return jnp.sum(jnp.sum(x, axis=0, keepdims=True), axis=1, keepdims=True)


def lane_row(values):
    lane = lax.broadcasted_iota(jnp.int32, (1, LANES), 1)
    out = jnp.zeros((1, LANES), jnp.float32)
    for i, v in enumerate(values):
        out = jnp.where(lane == i, v, out)
    return out


def prep_kernel(per_row, nsec, pad, owner_in, orders_in, source_in, psi_in, den_in, v_ref, v_out_ref, d_out_ref, slots_ref, owner_ref, orders_ref, source_ref, psi_ref, den_ref, sems):
    ends = ((owner_in, owner_ref), (orders_in, orders_ref), (source_in, source_ref), (psi_in, psi_ref), (den_in, den_ref))
    copies = [pltpu.make_async_copy(src, dst, sems.at[i]) for i, (src, dst) in enumerate(ends)]
    for c in copies:
        c.start()
    rows, width = psi_ref.shape[0], psi_ref.shape[2]
    lines = rows * per_row
    if pad > lines:
        for y in range(nsec):
            v_out_ref[y * pad + lines : (y + 1) * pad, :] = jnp.zeros((pad - lines, LANES), jnp.float32)
        d_out_ref[lines:pad, :] = jnp.ones((pad - lines, LANES), jnp.float32)
    row = lax.broadcasted_iota(jnp.int32, (rows, width), 0) + op_position() * rows
    col = lax.broadcasted_iota(jnp.int32, (rows, width), 1)
    for c in copies:
        c.wait()
    sector = sector_at(owner_ref, lax.axis_index("sec"), nsec)
    order = orders_ref[sector]
    for t in range(slots_ref.shape[0] - 1):
        slots_ref[t] = owner_ref[source_ref[sector, t]]
    slots_ref[slots_ref.shape[0] - 1] = order
    v = jnp.where((row < order) & (col < order), psi_ref[:, 0, :], 0.0)
    d = den_ref[:, 0, :]
    for k in range(per_row):
        part = slice(k * LANES, (k + 1) * LANES)
        at = pl.ds(k, rows, stride=per_row)
        v_ref[at, :] = v[:, part]
        d_out_ref[at, :] = d[:, part]
        for y in range(nsec):
            v_out_ref[pl.ds(y * pad + k, rows, stride=per_row), :] = v[:, part]


PIECES = 4


def spread(table_ref, slots_ref, out_ref, lines, pitch, buf_ref, sems):
    terms = out_ref.shape[0] // lines
    copies = []
    for c in range(PIECES):
        for t in range(c * terms // PIECES, (c + 1) * terms // PIECES):
            start = pl.multiple_of(slots_ref[t] * pitch, 8)
            buf_ref[t * lines : (t + 1) * lines, :] = table_ref[pl.ds(start, lines), :]
        at = pl.ds(c * (terms * lines // PIECES), terms * lines // PIECES)
        copies.append(pltpu.make_async_copy(buf_ref.at[at], out_ref.at[at], sems.at[c]))
        copies[-1].start()
    for c in copies:
        c.wait()


def select_kernel(lines, pad, slots_ref, v8_ref, out_ref, buf_ref, sems):
    spread(v8_ref, slots_ref, out_ref, lines, pad, buf_ref, sems)


def halves(x):
    hi = x.astype(jnp.bfloat16)
    return hi, (x - hi.astype(jnp.float32)).astype(jnp.bfloat16)


def dot3(a_hi, a_lo, b_hi, b_lo):
    dot = functools.partial(jnp.dot, preferred_element_type=jnp.float32)
    return dot(a_hi, b_hi) + (dot(a_hi, b_lo) + dot(a_lo, b_hi))


def split_rows(x_ref, hi_ref, lo_ref):
    step = 160

    def body(m, carry):
        at = pl.ds(pl.multiple_of(m * step, step), step)
        hi_ref[at, :], lo_ref[at, :] = halves(x_ref[at, :])
        return carry

    lax.fori_loop(0, x_ref.shape[0] // step, body, 0)


def split_kernel(rows, left_ref, right_ref, mats_ref, order_ref):
    width = left_ref.shape[0]
    half = width // 2
    mine = lax.axis_index("op_2") == 0
    for q in range(width // (2 * rows)):
        a = left_ref[2 * q * rows : (2 * q + 1) * rows, :]
        b = left_ref[(2 * q + 1) * rows : (2 * q + 2) * rows, :]
        order_ref[q * rows : (q + 1) * rows, :] = jnp.where(mine, b, a)
        order_ref[half + q * rows : half + (q + 1) * rows, :] = jnp.where(mine, a, b)
    split_rows(order_ref, mats_ref.at[0], mats_ref.at[1])
    split_rows(right_ref, mats_ref.at[2], mats_ref.at[3])


def left_product(mats_ref, ih_ref, il_ref, out_ref, first, per_row):
    step = 160
    for m in range(out_ref.shape[0] // per_row // step):
        at = pl.ds(first + m * step, step)
        y = dot3(mats_ref[0, at, :], mats_ref[1, at, :], ih_ref[...], il_ref[...])
        for k in range(per_row):
            out_ref[pl.ds(m * step * per_row + k, step, stride=per_row), :] = y[:, k * LANES : (k + 1) * LANES]


def inner_kernel(per_row, x_in, mats_ref, ih_ref, il_ref, out_ref, x_ref, sems):
    width = mats_ref.shape[1]
    step = width // PIECES
    copies = []
    for m in range(PIECES):
        at = pl.ds(m * step * per_row, step * per_row)
        copies.append(pltpu.make_async_copy(x_in.at[at], x_ref.at[at], sems.at[m]))
        copies[-1].start()
    for m in range(PIECES):
        copies[m].wait()
        x = jnp.concatenate(
            [x_ref[pl.ds(m * step * per_row + k, step, stride=per_row), :] for k in range(per_row)], axis=1
        )
        x_hi, x_lo = halves(x)
        at = pl.ds(m * step, step)
        ih_ref[at, :], il_ref[at, :] = halves(dot3(x_hi, x_lo, mats_ref[2], mats_ref[3]))
    left_product(mats_ref, ih_ref, il_ref, out_ref, 0, per_row)


def own_kernel(per_row, mats_ref, ih_ref, il_ref, out_ref):
    left_product(mats_ref, ih_ref, il_ref, out_ref, mats_ref.shape[1] // 2, per_row)


def masked_sum(part_ref, slots_ref, lines, per_row):
    parts = part_ref.shape[0] // lines
    w = part_ref[0:lines, :]
    for q in range(1, parts):
        w = w + part_ref[q * lines : (q + 1) * lines, :]
    keep = row_mask(slots_ref[slots_ref.shape[0] - 1], lines, per_row, op_position() * (lines // per_row))
    return jnp.where(keep, w, 0.0)


def share_kernel(lines, pad, per_row, nsec, slots_ref, part_ref, w_ref, out_ref):
    w = masked_sum(part_ref, slots_ref, lines, per_row)
    w_ref[...] = w
    for y in range(nsec):
        out_ref[y * pad : y * pad + lines, :] = w
        if pad > lines:
            out_ref[y * pad + lines : (y + 1) * pad, :] = jnp.zeros((pad - lines, LANES), jnp.float32)


def first_sums_kernel(pad, nsec, v8_ref, w8_ref, out_ref):
    vv = jnp.zeros((pad, LANES), jnp.float32)
    vw = jnp.zeros((pad, LANES), jnp.float32)
    for y in range(nsec):
        v = v8_ref[y * pad : (y + 1) * pad, :]
        vv = vv + v * v
        vw = vw + v * w8_ref[y * pad : (y + 1) * pad, :]
    out_ref[...] = jnp.broadcast_to(lane_row([total(vv), total(vw)]), out_ref.shape)


def update_kernel(lines, pad, nsec, count, slots_ref, sums_ref, v8_ref, d8_ref, w8_ref, out_ref, t_ref, scal_ref, t8_ref, buf_ref, sems):
    sums = jnp.sum(sums_ref[...], axis=0, keepdims=True) / count
    norm, product = sums[:, 0:1], sums[:, 1:2]
    scale = 1.0 / jnp.sqrt(norm + EPS)
    rayleigh = product / (norm + EPS)
    me = lax.axis_index("sec")
    for k in range(nsec):
        slot = lax.rem(me + nsec - k, nsec)
        at = pl.ds(pl.multiple_of(slot * pad, 8), pad)
        t8_ref[at, :] = (scale * w8_ref[at, :] - rayleigh * (scale * v8_ref[at, :])) / d8_ref[k * pad : (k + 1) * pad, :]
    t_ref[...] = t8_ref[pl.ds(pl.multiple_of(me * pad, 8), lines), :]
    scal_ref[...] = jnp.broadcast_to(lane_row([norm, product]), scal_ref.shape)
    spread(t8_ref, slots_ref, out_ref, lines, pad, buf_ref, sems)


def last_sums_kernel(lines, per_row, pad, slots_ref, part_ref, scal_ref, v_ref, w_ref, t_ref, d_ref, out_ref, keep_ref):
    h = masked_sum(part_ref, slots_ref, lines, per_row)
    scale = 1.0 / jnp.sqrt(scal_ref[0:1, 0:1] + EPS)
    v0 = scale * v_ref[...]
    w0 = scale * w_ref[...]
    t = t_ref[...]
    for i, x in enumerate((v0, w0, t, h, d_ref[0:lines, :])):
        keep_ref[i * pad : i * pad + lines, :] = x
    keep_ref[5 * pad : 5 * pad + 8, :] = scal_ref[...]
    out_ref[...] = lane_row([total(v0 * t), total(t * t), total(t * w0), total(t * h), total(v0 * h)])


def final_kernel(count, per_row, lines, pad, sums_ref, keep_ref, new_ref, corr_ref, new_lines, corr_lines):
    norm, product = keep_ref[5 * pad : 5 * pad + 1, 0:1], keep_ref[5 * pad : 5 * pad + 1, 1:2]
    v0, w0, t, h, d = (keep_ref[i * pad : i * pad + lines, :] for i in range(5))
    sums = jnp.sum(sums_ref[...], axis=0, keepdims=True) / count
    along, tt, tw, th, vh = (sums[:, i : i + 1] for i in range(5))
    rayleigh = product / (norm + EPS)
    vv = norm / (norm + EPS)
    tail = tt - 2.0 * along * along + along * along * vv
    inv = 1.0 / jnp.sqrt(tail + EPS)
    corner = inv * inv * (th - along * (tw + vh) + along * along * rayleigh)
    couple = inv * (tw - along * rayleigh)
    y = 2.0 * couple
    x = rayleigh - corner
    big = jnp.maximum(jnp.abs(x), jnp.abs(y))
    none = big == 0.0
    big = jnp.where(none, 1.0, big)
    xs = jnp.where(none, 1.0, x / big)
    ys = y / big
    hyp = jnp.sqrt(xs * xs + ys * ys)
    major = jnp.sqrt((hyp + jnp.abs(xs)) / (2.0 * hyp))
    minor = jnp.abs(ys) / (2.0 * hyp * major)
    ahead = xs > 0.0
    cosine = jnp.where(ahead, major, minor)
    sine = jnp.where(ys < 0.0, -1.0, 1.0) * jnp.where(ahead, minor, major)
    v1 = inv * (t - along * v0)
    w1 = inv * (h - along * w0)
    new = sine * v0 - cosine * v1
    applied = sine * w0 - cosine * w1
    lam = sine * sine * rayleigh + cosine * cosine * corner - 2.0 * sine * cosine * couple
    new_lines[...] = new
    corr_lines[...] = (applied - lam * new) / d
    rows = new_ref.shape[0]
    for k in range(per_row):
        at, part = pl.ds(k, rows, stride=per_row), slice(k * LANES, (k + 1) * LANES)
        new_ref[:, 0, part] = new_lines[at, :]
        corr_ref[:, 0, part] = corr_lines[at, :]


def f32(*shape):
    return jax.ShapeDtypeStruct(shape, jnp.float32)


def bf16(*shape):
    return jax.ShapeDtypeStruct(shape, jnp.bfloat16)


def call(kernel, out, smem, vmem, scratch=(), anywhere=(), out_anywhere=0, out_smem=0, limit=32 * 1024 * 1024):
    outs = out if isinstance(out, tuple) else (out,)
    specs = [ANY] * out_anywhere + [VMEM] * (len(outs) - out_anywhere - out_smem) + [SMEM] * out_smem
    return pl.pallas_call(
        kernel,
        out_shape=out,
        in_specs=[SMEM] * len(smem) + [ANY] * len(anywhere) + [VMEM] * len(vmem),
        out_specs=tuple(specs) if isinstance(out, tuple) else specs[0],
        scratch_shapes=scratch,
        compiler_params=pltpu.CompilerParams(vmem_limit_bytes=limit),
    )(*smem, *anywhere, *vmem)


def exchange(x, axis, parts):
    lines = x.shape[0] // parts
    y = lax.all_to_all(x.reshape(parts, lines, 1, LANES), axis, 0, 0, tiled=True)
    return y.reshape(x.shape)


def per_device(psi, left_env, right_env, denominators, source_sector, owner, orders):
    rows = psi.shape[0]
    width = psi.shape[2]
    per_row = width // LANES
    lines = rows * per_row
    pad = up8(lines)
    nop = lax.axis_size(OP)
    nchip = lax.axis_size(CHIP)
    nsec = lax.axis_size("sec")
    count = float(width * nsec * width)
    left = left_env.reshape(width, width)
    right = right_env.reshape(width, width)
    source = source_sector.T
    part = functools.partial
    swap = [(0, 1), (1, 0)]

    v, v_out, d_out, slots = call(
        part(prep_kernel, per_row, nsec, pad),
        (
            f32(lines, LANES),
            f32(nsec * pad, LANES),
            f32(pad, LANES),
            jax.ShapeDtypeStruct((nop + 1,), jnp.int32),
        ),
        (),
        (),
        limit=None,
        out_smem=1,
        anywhere=(owner, orders, source, psi, denominators),
        scratch=[
            pltpu.SMEM((nsec,), jnp.int32),
            pltpu.SMEM((nsec,), jnp.int32),
            pltpu.SMEM(source.shape, jnp.int32),
            pltpu.VMEM(psi.shape, jnp.float32),
            pltpu.VMEM(psi.shape, jnp.float32),
            pltpu.SemaphoreType.DMA((5,)),
        ],
    )
    v8 = exchange(v_out, "sec", nsec)
    square = bf16(width, width)
    half = f32(width * per_row // 2, LANES)
    mats = call(
        part(split_kernel, rows),
        bf16(4, width, width),
        (),
        (left, right),
        scratch=[pltpu.VMEM((width, width), jnp.float32)],
    )

    whole = [pltpu.VMEM((nop * lines, LANES), jnp.float32), pltpu.SemaphoreType.DMA((PIECES,))]

    def products(x):
        ih, il, other = call(
            part(inner_kernel, per_row), (square, square, half), (), (mats,), anywhere=(x,), scratch=whole
        )
        came = lax.ppermute(other, "op_2", swap)
        own = call(part(own_kernel, per_row), half, (), (mats, ih, il))
        return exchange(own + came, CHIP, nchip)

    chosen = call(
        part(select_kernel, lines, pad),
        f32(nop * lines, LANES),
        (slots,),
        (v8,),
        scratch=whole,
        out_anywhere=1,
    )
    chosen, d8 = lax.optimization_barrier((chosen, d_out))
    chosen = exchange(chosen, OP, nop)
    reach = 1
    while reach < nsec:
        came = lax.ppermute(d8, "sec", [(i, (i + reach) % nsec) for i in range(nsec)])
        d8 = jnp.concatenate([d8, came], axis=0)
        reach *= 2
    chosen, d8 = lax.optimization_barrier((chosen, d8))
    parts = products(chosen)
    w, w_out = call(
        part(share_kernel, lines, pad, per_row, nsec),
        (f32(lines, LANES), f32(nsec * pad, LANES)),
        (slots,),
        (parts,),
    )
    w8 = exchange(w_out, "sec", nsec)
    sums = call(part(first_sums_kernel, pad, nsec), f32(nop, LANES), (), (v8, w8))
    sums = exchange(sums, OP, nop)
    chosen, t, scal = call(
        part(update_kernel, lines, pad, nsec, count),
        (f32(nop * lines, LANES), f32(lines, LANES), f32(8, LANES)),
        (slots,),
        (sums, v8, d8, w8),
        scratch=[pltpu.VMEM((nsec * pad, LANES), jnp.float32), *whole],
        out_anywhere=1,
    )
    parts = products(exchange(chosen, OP, nop))
    sums, keep = call(
        part(last_sums_kernel, lines, per_row, pad),
        (f32(1, LANES), f32(5 * pad + 8, LANES)),
        (slots,),
        (parts, scal, v, w, t, d_out),
    )
    chips = nchip * nsec
    sums = jnp.broadcast_to(lax.psum(sums, "op_2"), (chips, LANES))
    sums = exchange(sums, (*CHIP, "sec"), chips)
    return call(
        part(final_kernel, count, per_row, lines, pad),
        (f32(*psi.shape), f32(*psi.shape)),
        (),
        (sums, keep),
        scratch=[pltpu.VMEM((lines, LANES), jnp.float32)] * 2,
    )


def solution(mesh):
    sec = mesh.shape["sec"]
    torus = Mesh(mesh.devices.reshape(4, 8, 2, sec), (*OP, "sec"))
    specs = (
        P(OP, "sec", None),
        P(OP, "sec", None, None),
        P(OP, "sec", None, None),
        P(OP, "sec", None),
        P(),
        P(),
        P(),
    )
    outs = (P(OP, "sec", None), P(OP, "sec", None))
    return jax.shard_map(per_device, mesh=torus, in_specs=specs, out_specs=outs, check_vma=False)
```

```python
import functools

import jax
import jax.numpy as jnp
from jax import lax
from jax.experimental import pallas as pl
from jax.experimental.pallas import tpu as pltpu
from jax.sharding import Mesh
from jax.sharding import PartitionSpec as P

OP = ("op_0", "op_1", "op_2")
EPS = 1e-06
LANES = 128
VMEM = pl.BlockSpec(memory_space=pltpu.VMEM)
SMEM = pl.BlockSpec(memory_space=pltpu.SMEM)
ANY = pl.BlockSpec(memory_space=pl.ANY)


def up8(n):
    return -(-n // 8) * 8


def op_position():
    sizes = [lax.axis_size(a) for a in OP]
    return (lax.axis_index("op_0") * sizes[1] + lax.axis_index("op_1")) * sizes[2] + lax.axis_index("op_2")


def sector_at(owner_ref, slot, nsec):
    found = jnp.int32(0)
    for s in range(nsec):
        found = found + jnp.where(owner_ref[s] == slot, s, 0)
    return found


def row_mask(order, lines, per_row, first_row):
    line = lax.broadcasted_iota(jnp.int32, (lines, LANES), 0)
    lane = lax.broadcasted_iota(jnp.int32, (lines, LANES), 1)
    row = line // per_row
    col = (line - row * per_row) * LANES + lane
    return (first_row + row < order) & (col < order)


def total(x):
    return jnp.sum(jnp.sum(x, axis=0, keepdims=True), axis=1, keepdims=True)


def lane_row(values):
    lane = lax.broadcasted_iota(jnp.int32, (1, LANES), 1)
    out = jnp.zeros((1, LANES), jnp.float32)
    for i, v in enumerate(values):
        out = jnp.where(lane == i, v, out)
    return out


def prep_kernel(per_row, nsec, pad, owner_in, orders_in, source_in, psi_in, den_in, v_ref, v_out_ref, d_out_ref, slots_ref, owner_ref, orders_ref, source_ref, psi_ref, den_ref, sems):
    ends = ((owner_in, owner_ref), (orders_in, orders_ref), (source_in, source_ref), (psi_in, psi_ref), (den_in, den_ref))
    copies = [pltpu.make_async_copy(src, dst, sems.at[i]) for i, (src, dst) in enumerate(ends)]
    for c in copies:
        c.start()
    rows, width = psi_ref.shape[0], psi_ref.shape[2]
    lines = rows * per_row
    if pad > lines:
        for y in range(nsec):
            v_out_ref[y * pad + lines : (y + 1) * pad, :] = jnp.zeros((pad - lines, LANES), jnp.float32)
        d_out_ref[lines:pad, :] = jnp.ones((pad - lines, LANES), jnp.float32)
        v_ref[lines:pad, :] = jnp.zeros((pad - lines, LANES), jnp.float32)
    row = lax.broadcasted_iota(jnp.int32, (rows, width), 0) + op_position() * rows
    col = lax.broadcasted_iota(jnp.int32, (rows, width), 1)
    for c in copies:
        c.wait()
    sector = sector_at(owner_ref, lax.axis_index("sec"), nsec)
    order = orders_ref[sector]
    for t in range(slots_ref.shape[0] - 1):
        slots_ref[t] = owner_ref[source_ref[sector, t]]
    slots_ref[slots_ref.shape[0] - 1] = order
    v = jnp.where((row < order) & (col < order), psi_ref[:, 0, :], 0.0)
    d = den_ref[:, 0, :]
    for k in range(per_row):
        part = slice(k * LANES, (k + 1) * LANES)
        at = pl.ds(k, rows, stride=per_row)
        v_ref[at, :] = v[:, part]
        d_out_ref[at, :] = d[:, part]
        for y in range(nsec):
            v_out_ref[pl.ds(y * pad + k, rows, stride=per_row), :] = v[:, part]


PIECES = 4


def spread(table_ref, slots_ref, out_ref, lines, pitch, buf_ref, sems):
    terms = out_ref.shape[0] // lines
    copies = []
    for c in range(PIECES):
        for t in range(c * terms // PIECES, (c + 1) * terms // PIECES):
            start = pl.multiple_of(slots_ref[t] * pitch, 8)
            buf_ref[t * lines : (t + 1) * lines, :] = table_ref[pl.ds(start, lines), :]
        at = pl.ds(c * (terms * lines // PIECES), terms * lines // PIECES)
        copies.append(pltpu.make_async_copy(buf_ref.at[at], out_ref.at[at], sems.at[c]))
        copies[-1].start()
    for c in copies:
        c.wait()


def select_kernel(lines, pad, slots_ref, v8_ref, out_ref, buf_ref, sems):
    spread(v8_ref, slots_ref, out_ref, lines, pad, buf_ref, sems)


def halves(x):
    hi = x.astype(jnp.bfloat16)
    return hi, (x - hi.astype(jnp.float32)).astype(jnp.bfloat16)


def dot3(a_hi, a_lo, b_hi, b_lo):
    dot = functools.partial(jnp.dot, preferred_element_type=jnp.float32)
    return dot(a_hi, b_hi) + (dot(a_hi, b_lo) + dot(a_lo, b_hi))


def split_rows(x_ref, hi_ref, lo_ref):
    step = 160

    def body(m, carry):
        at = pl.ds(pl.multiple_of(m * step, step), step)
        hi_ref[at, :], lo_ref[at, :] = halves(x_ref[at, :])
        return carry

    lax.fori_loop(0, x_ref.shape[0] // step, body, 0)


def split_kernel(rows, left_ref, right_ref, mats_ref, order_ref):
    width = left_ref.shape[0]
    half = width // 2
    mine = lax.axis_index("op_2") == 0
    for q in range(width // (2 * rows)):
        a = left_ref[2 * q * rows : (2 * q + 1) * rows, :]
        b = left_ref[(2 * q + 1) * rows : (2 * q + 2) * rows, :]
        order_ref[q * rows : (q + 1) * rows, :] = jnp.where(mine, b, a)
        order_ref[half + q * rows : half + (q + 1) * rows, :] = jnp.where(mine, a, b)
    split_rows(order_ref, mats_ref.at[0], mats_ref.at[1])
    split_rows(right_ref, mats_ref.at[2], mats_ref.at[3])


def left_product(mats_ref, ih_ref, il_ref, out_ref, first, per_row):
    step = 160
    for m in range(out_ref.shape[0] // per_row // step):
        at = pl.ds(first + m * step, step)
        y = dot3(mats_ref[0, at, :], mats_ref[1, at, :], ih_ref[...], il_ref[...])
        for k in range(per_row):
            out_ref[pl.ds(m * step * per_row + k, step, stride=per_row), :] = y[:, k * LANES : (k + 1) * LANES]


def inner_kernel(per_row, x_ref, mats_ref, ih_ref, il_ref, out_ref):
    width = mats_ref.shape[1]
    step = 160
    for m in range(width // step):
        x = jnp.concatenate(
            [x_ref[pl.ds(m * step * per_row + k, step, stride=per_row), :] for k in range(per_row)], axis=1
        )
        x_hi, x_lo = halves(x)
        at = pl.ds(m * step, step)
        ih_ref[at, :], il_ref[at, :] = halves(dot3(x_hi, x_lo, mats_ref[2], mats_ref[3]))
    left_product(mats_ref, ih_ref, il_ref, out_ref, 0, per_row)


def own_kernel(per_row, mats_ref, ih_ref, il_ref, out_ref):
    left_product(mats_ref, ih_ref, il_ref, out_ref, mats_ref.shape[1] // 2, per_row)


def ring_slot(k, count):
    ahead = count // 2
    shift = -k if k <= ahead else k - ahead
    return lax.rem(lax.axis_index("op_1") + shift + count, count)


def fold(part_ref, out_ref, lines, pad, nz):
    nx = part_ref.shape[0] // (nz * lines)
    for z in range(nz):
        x = part_ref[z * lines : (z + 1) * lines, :]
        for i in range(1, nx):
            x = x + part_ref[(i * nz + z) * lines : (i * nz + z + 1) * lines, :]
        out_ref[z * pad : z * pad + lines, :] = x
        out_ref[z * pad + lines : (z + 1) * pad, :] = jnp.zeros((pad - lines, LANES), jnp.float32)


def ring_dot(ring, out_ref, lines, pad):
    acc = jnp.zeros((lines, LANES), jnp.float32)
    for k, ref in enumerate(ring):
        at = pl.ds(pl.multiple_of(ring_slot(k, len(ring)) * pad, 8), lines)
        acc = acc + ref[0:lines, :] * out_ref[at, :]
    return total(acc)


def put_line(out_ref, row, lines, pad):
    for b in range(out_ref.shape[0] // pad):
        out_ref[b * pad + lines : b * pad + lines + 1, :] = row


def first_fold_kernel(lines, pad, nz, part_ref, *refs):
    ring, out_ref = refs[:nz], refs[nz]
    fold(part_ref, out_ref, lines, pad, nz)
    own = ring[0][...]
    put_line(out_ref, lane_row([total(own * own), ring_dot(ring, out_ref, lines, pad)]), lines, pad)


def masked_sum(msg_ref, slots_ref, lines, pad, per_row):
    w = msg_ref[0:pad, :]
    for q in range(1, msg_ref.shape[0] // pad):
        w = w + msg_ref[q * pad : (q + 1) * pad, :]
    keep = row_mask(slots_ref[slots_ref.shape[0] - 1], lines, per_row, op_position() * (lines // per_row))
    return jnp.where(keep, w[0:lines, :], 0.0), w[lines : lines + 1, :]


def share_kernel(lines, pad, per_row, nsec, slots_ref, msg_ref, w_ref, out_ref):
    w, row = masked_sum(msg_ref, slots_ref, lines, pad, per_row)
    w_ref[...] = w
    for y in range(nsec):
        out_ref[y * pad : y * pad + lines, :] = w
        out_ref[y * pad + lines : (y + 1) * pad, :] = jnp.zeros((pad - lines, LANES), jnp.float32)
    put_line(out_ref, row, lines, pad)


def first_sums_kernel(lines, pad, w8_ref, out_ref):
    row = w8_ref[lines : lines + 1, :]
    for y in range(1, w8_ref.shape[0] // pad):
        row = row + w8_ref[y * pad + lines : y * pad + lines + 1, :]
    out_ref[...] = jnp.broadcast_to(row, out_ref.shape)


def update_kernel(lines, pad, nsec, count, slots_ref, sums_ref, v8_ref, d8_ref, w8_ref, out_ref, t_ref, scal_ref, t8_ref, buf_ref, sems):
    sums = jnp.sum(sums_ref[...], axis=0, keepdims=True) / count
    norm, product = sums[:, 0:1], sums[:, 1:2]
    scale = 1.0 / jnp.sqrt(norm + EPS)
    rayleigh = product / (norm + EPS)
    me = lax.axis_index("sec")
    for k in range(nsec):
        slot = lax.rem(me + nsec - k, nsec)
        at = pl.ds(pl.multiple_of(slot * pad, 8), pad)
        t8_ref[at, :] = (scale * w8_ref[at, :] - rayleigh * (scale * v8_ref[at, :])) / d8_ref[k * pad : (k + 1) * pad, :]
    t_ref[...] = t8_ref[pl.ds(pl.multiple_of(me * pad, 8), pad), :]
    scal_ref[...] = jnp.broadcast_to(lane_row([norm, product]), scal_ref.shape)
    spread(t8_ref, slots_ref, out_ref, lines, pad, buf_ref, sems)


def last_fold_kernel(lines, pad, nz, part_ref, scal_ref, w_ref, *refs):
    v_ring, t_ring, out_ref = refs[:nz], refs[nz : 2 * nz], refs[2 * nz]
    fold(part_ref, out_ref, lines, pad, nz)
    scale = 1.0 / jnp.sqrt(scal_ref[0:1, 0:1] + EPS)
    v0 = scale * v_ring[0][0:lines, :]
    w0 = scale * w_ref[...]
    t = t_ring[0][0:lines, :]
    th = ring_dot(t_ring, out_ref, lines, pad)
    vh = scale * ring_dot(v_ring, out_ref, lines, pad)
    put_line(out_ref, lane_row([total(v0 * t), total(t * t), total(t * w0), th, vh]), lines, pad)


def last_sums_kernel(lines, per_row, pad, slots_ref, msg_ref, scal_ref, v_ref, w_ref, t_ref, d_ref, out_ref, keep_ref):
    h, row = masked_sum(msg_ref, slots_ref, lines, pad, per_row)
    scale = 1.0 / jnp.sqrt(scal_ref[0:1, 0:1] + EPS)
    for i, x in enumerate((scale * v_ref[0:lines, :], scale * w_ref[...], t_ref[0:lines, :], h, d_ref[0:lines, :])):
        keep_ref[i * pad : i * pad + lines, :] = x
    keep_ref[5 * pad : 5 * pad + 8, :] = scal_ref[...]
    out_ref[...] = jnp.broadcast_to(row, out_ref.shape)


def final_kernel(count, per_row, lines, pad, sums_ref, keep_ref, new_ref, corr_ref, new_lines, corr_lines):
    norm, product = keep_ref[5 * pad : 5 * pad + 1, 0:1], keep_ref[5 * pad : 5 * pad + 1, 1:2]
    v0, w0, t, h, d = (keep_ref[i * pad : i * pad + lines, :] for i in range(5))
    sums = jnp.sum(sums_ref[...], axis=0, keepdims=True) / count
    along, tt, tw, th, vh = (sums[:, i : i + 1] for i in range(5))
    rayleigh = product / (norm + EPS)
    vv = norm / (norm + EPS)
    tail = tt - 2.0 * along * along + along * along * vv
    inv = 1.0 / jnp.sqrt(tail + EPS)
    corner = inv * inv * (th - along * (tw + vh) + along * along * rayleigh)
    couple = inv * (tw - along * rayleigh)
    y = 2.0 * couple
    x = rayleigh - corner
    big = jnp.maximum(jnp.abs(x), jnp.abs(y))
    none = big == 0.0
    big = jnp.where(none, 1.0, big)
    xs = jnp.where(none, 1.0, x / big)
    ys = y / big
    hyp = jnp.sqrt(xs * xs + ys * ys)
    major = jnp.sqrt((hyp + jnp.abs(xs)) / (2.0 * hyp))
    minor = jnp.abs(ys) / (2.0 * hyp * major)
    ahead = xs > 0.0
    cosine = jnp.where(ahead, major, minor)
    sine = jnp.where(ys < 0.0, -1.0, 1.0) * jnp.where(ahead, minor, major)
    v1 = inv * (t - along * v0)
    w1 = inv * (h - along * w0)
    new = sine * v0 - cosine * v1
    applied = sine * w0 - cosine * w1
    lam = sine * sine * rayleigh + cosine * cosine * corner - 2.0 * sine * cosine * couple
    new_lines[...] = new
    corr_lines[...] = (applied - lam * new) / d
    rows = new_ref.shape[0]
    for k in range(per_row):
        at, part = pl.ds(k, rows, stride=per_row), slice(k * LANES, (k + 1) * LANES)
        new_ref[:, 0, part] = new_lines[at, :]
        corr_ref[:, 0, part] = corr_lines[at, :]


def f32(*shape):
    return jax.ShapeDtypeStruct(shape, jnp.float32)


def bf16(*shape):
    return jax.ShapeDtypeStruct(shape, jnp.bfloat16)


def call(kernel, out, smem, vmem, scratch=(), anywhere=(), out_anywhere=0, out_smem=0, limit=32 * 1024 * 1024):
    outs = out if isinstance(out, tuple) else (out,)
    specs = [ANY] * out_anywhere + [VMEM] * (len(outs) - out_anywhere - out_smem) + [SMEM] * out_smem
    return pl.pallas_call(
        kernel,
        out_shape=out,
        in_specs=[SMEM] * len(smem) + [ANY] * len(anywhere) + [VMEM] * len(vmem),
        out_specs=tuple(specs) if isinstance(out, tuple) else specs[0],
        scratch_shapes=scratch,
        compiler_params=pltpu.CompilerParams(vmem_limit_bytes=limit),
    )(*smem, *anywhere, *vmem)


def exchange(x, axis, parts):
    lines = x.shape[0] // parts
    y = lax.all_to_all(x.reshape(parts, lines, 1, LANES), axis, 0, 0, tiled=True)
    return y.reshape(x.shape)


def per_device(psi, left_env, right_env, denominators, source_sector, owner, orders):
    rows = psi.shape[0]
    width = psi.shape[2]
    per_row = width // LANES
    lines = rows * per_row
    pad = up8(lines + 1)
    nop = lax.axis_size(OP)
    nx = lax.axis_size("op_0")
    nz = lax.axis_size("op_1")
    nsec = lax.axis_size("sec")
    count = float(width * nsec * width)
    left = left_env.reshape(width, width)
    right = right_env.reshape(width, width)
    source = source_sector.T
    part = functools.partial
    swap = [(0, 1), (1, 0)]

    v, v_out, d_out, slots = call(
        part(prep_kernel, per_row, nsec, pad),
        (
            f32(pad, LANES),
            f32(nsec * pad, LANES),
            f32(pad, LANES),
            jax.ShapeDtypeStruct((nop + 1,), jnp.int32),
        ),
        (),
        (),
        limit=None,
        out_smem=1,
        anywhere=(owner, orders, source, psi, denominators),
        scratch=[
            pltpu.SMEM((nsec,), jnp.int32),
            pltpu.SMEM((nsec,), jnp.int32),
            pltpu.SMEM(source.shape, jnp.int32),
            pltpu.VMEM(psi.shape, jnp.float32),
            pltpu.VMEM(psi.shape, jnp.float32),
            pltpu.SemaphoreType.DMA((5,)),
        ],
    )
    v8 = exchange(v_out, "sec", nsec)
    square = bf16(width, width)
    half = f32(width * per_row // 2, LANES)
    mats = call(
        part(split_kernel, rows),
        bf16(4, width, width),
        (),
        (left, right),
        scratch=[pltpu.VMEM((width, width), jnp.float32)],
    )

    whole = [pltpu.VMEM((nop * lines, LANES), jnp.float32), pltpu.SemaphoreType.DMA((PIECES,))]

    def products(x):
        ih, il, other = call(part(inner_kernel, per_row), (square, square, half), (), (x, mats))
        came = lax.ppermute(other, "op_2", swap)
        own = call(part(own_kernel, per_row), half, (), (mats, ih, il))
        return exchange(own + came, "op_0", nx)

    def round_z(x):
        ahead, behind = [x], [x]
        for _ in range(nz // 2):
            ahead.append(lax.ppermute(ahead[-1], "op_1", [(i, (i + 1) % nz) for i in range(nz)]))
        for _ in range((nz - 1) // 2):
            behind.append(lax.ppermute(behind[-1], "op_1", [(i, (i - 1) % nz) for i in range(nz)]))
        return ahead + behind[1:]

    chosen = call(
        part(select_kernel, lines, pad),
        f32(nop * lines, LANES),
        (slots,),
        (v8,),
        scratch=whole,
        out_anywhere=1,
    )
    chosen, d8, v = lax.optimization_barrier((chosen, d_out, v))
    chosen = exchange(chosen, OP, nop)
    reach = 1
    while reach < nsec:
        came = lax.ppermute(d8, "sec", [(i, (i + reach) % nsec) for i in range(nsec)])
        d8 = jnp.concatenate([d8, came], axis=0)
        reach *= 2
    chosen, d8, *v_ring = lax.optimization_barrier((chosen, d8, *round_z(v)))
    parts = products(chosen)
    sums = call(part(first_fold_kernel, lines, pad, nz), f32(nz * pad, LANES), (), (parts, *v_ring))
    w, w_out = call(
        part(share_kernel, lines, pad, per_row, nsec),
        (f32(lines, LANES), f32(nsec * pad, LANES)),
        (slots,),
        (exchange(sums, "op_1", nz),),
    )
    w8 = exchange(w_out, "sec", nsec)
    near = ("op_0", "op_2")
    count_near = lax.axis_size(near)
    sums = call(part(first_sums_kernel, lines, pad), f32(count_near, LANES), (), (w8,))
    sums = exchange(sums, near, count_near)
    chosen, t, scal = call(
        part(update_kernel, lines, pad, nsec, count),
        (f32(nop * lines, LANES), f32(pad, LANES), f32(8, LANES)),
        (slots,),
        (sums, v8, d8, w8),
        limit=52 * 1024 * 1024,
        scratch=[pltpu.VMEM((nsec * pad, LANES), jnp.float32), *whole],
        out_anywhere=1,
    )
    chosen, *t_ring = lax.optimization_barrier((exchange(chosen, OP, nop), *round_z(t)))
    parts = products(chosen)
    sums = call(
        part(last_fold_kernel, lines, pad, nz),
        f32(nz * pad, LANES),
        (),
        (parts, scal, w, *v_ring, *t_ring),
    )
    near = ("op_0", "op_2", "sec")
    count_near = lax.axis_size(near)
    sums, keep = call(
        part(last_sums_kernel, lines, per_row, pad),
        (f32(count_near, LANES), f32(5 * pad + 8, LANES)),
        (slots,),
        (exchange(sums, "op_1", nz), scal, v, w, t, d_out),
    )
    return call(
        part(final_kernel, count, per_row, lines, pad),
        (f32(*psi.shape), f32(*psi.shape)),
        (),
        (exchange(sums, near, count_near), keep),
        scratch=[pltpu.VMEM((lines, LANES), jnp.float32)] * 2,
    )


def solution(mesh):
    sec = mesh.shape["sec"]
    torus = Mesh(mesh.devices.reshape(4, 8, 2, sec), (*OP, "sec"))
    specs = (
        P(OP, "sec", None),
        P(OP, "sec", None, None),
        P(OP, "sec", None, None),
        P(OP, "sec", None),
        P(),
        P(),
        P(),
    )
    outs = (P(OP, "sec", None), P(OP, "sec", None))
    return jax.shard_map(per_device, mesh=torus, in_specs=specs, out_specs=outs, check_vma=False)
```

```python
import functools

import jax
import jax.numpy as jnp
from jax import lax
from jax.experimental import pallas as pl
from jax.experimental.pallas import tpu as pltpu
from jax.sharding import Mesh
from jax.sharding import PartitionSpec as P

CHIP = ("op_0", "op_1")
OP = ("op_0", "op_1", "op_2")
EPS = 1e-06
LANES = 128
VMEM = pl.BlockSpec(memory_space=pltpu.VMEM)
SMEM = pl.BlockSpec(memory_space=pltpu.SMEM)
ANY = pl.BlockSpec(memory_space=pl.ANY)


def up8(n):
    return -(-n // 8) * 8


def op_position():
    sizes = [lax.axis_size(a) for a in OP]
    return (lax.axis_index("op_0") * sizes[1] + lax.axis_index("op_1")) * sizes[2] + lax.axis_index("op_2")


def sector_at(owner_ref, slot, nsec):
    found = jnp.int32(0)
    for s in range(nsec):
        found = found + jnp.where(owner_ref[s] == slot, s, 0)
    return found


def row_mask(order, lines, per_row, first_row):
    line = lax.broadcasted_iota(jnp.int32, (lines, LANES), 0)
    lane = lax.broadcasted_iota(jnp.int32, (lines, LANES), 1)
    row = line // per_row
    col = (line - row * per_row) * LANES + lane
    return (first_row + row < order) & (col < order)


def total(x):
    return jnp.sum(jnp.sum(x, axis=0, keepdims=True), axis=1, keepdims=True)


def lane_row(values):
    lane = lax.broadcasted_iota(jnp.int32, (1, LANES), 1)
    out = jnp.zeros((1, LANES), jnp.float32)
    for i, v in enumerate(values):
        out = jnp.where(lane == i, v, out)
    return out


def prep_kernel(per_row, nsec, pad, owner_in, orders_in, source_in, psi_in, den_in, v_ref, v_out_ref, d_out_ref, slots_ref, owner_ref, orders_ref, source_ref, psi_ref, den_ref, sems):
    ends = ((owner_in, owner_ref), (orders_in, orders_ref), (source_in, source_ref), (psi_in, psi_ref), (den_in, den_ref))
    copies = [pltpu.make_async_copy(src, dst, sems.at[i]) for i, (src, dst) in enumerate(ends)]
    for c in copies:
        c.start()
    rows, width = psi_ref.shape[0], psi_ref.shape[2]
    lines = rows * per_row
    if pad > lines:
        d_out_ref[lines:pad, :] = jnp.ones((pad - lines, LANES), jnp.float32)
    row = lax.broadcasted_iota(jnp.int32, (rows, width), 0) + op_position() * rows
    col = lax.broadcasted_iota(jnp.int32, (rows, width), 1)
    for c in copies:
        c.wait()
    sector = sector_at(owner_ref, lax.axis_index("sec"), nsec)
    order = orders_ref[sector]
    for t in range(slots_ref.shape[0] - 1):
        slots_ref[t] = owner_ref[source_ref[sector, t]]
    slots_ref[slots_ref.shape[0] - 1] = order
    v = jnp.where((row < order) & (col < order), psi_ref[:, 0, :], 0.0)
    d = den_ref[:, 0, :]
    for k in range(per_row):
        part = slice(k * LANES, (k + 1) * LANES)
        at = pl.ds(k, rows, stride=per_row)
        v_ref[at, :] = v[:, part]
        d_out_ref[at, :] = d[:, part]
        for y in range(nsec):
            v_out_ref[pl.ds(y * lines + k, rows, stride=per_row), :] = v[:, part]


PIECES = 4


def pick(table_ref, slots_ref, t, lines, pitch):
    return table_ref[pl.ds(pl.multiple_of(slots_ref[t] * pitch, 8), lines), :]


def select_kernel(lines, pad, nsec, slots_ref, v8_ref, out_ref, table_ref, buf_ref, sems):
    for y in range(nsec):
        table_ref[y * pad : y * pad + lines, :] = v8_ref[y * lines : (y + 1) * lines, :]
    terms = out_ref.shape[0] // lines
    copies = []
    for c in range(PIECES):
        for t in range(c * terms // PIECES, (c + 1) * terms // PIECES):
            buf_ref[t * lines : (t + 1) * lines, :] = pick(table_ref, slots_ref, t, lines, pad)
        at = pl.ds(c * (terms * lines // PIECES), terms * lines // PIECES)
        copies.append(pltpu.make_async_copy(buf_ref.at[at], out_ref.at[at], sems.at[c]))
        copies[-1].start()
    for c in copies:
        c.wait()


def halves(x):
    hi = x.astype(jnp.bfloat16)
    return hi, (x - hi.astype(jnp.float32)).astype(jnp.bfloat16)


def dot3(a_hi, a_lo, b_hi, b_lo):
    dot = functools.partial(jnp.dot, preferred_element_type=jnp.float32)
    return dot(a_hi, b_hi) + (dot(a_hi, b_lo) + dot(a_lo, b_hi))


def split_rows(x_ref, hi_ref, lo_ref):
    step = 160

    def body(m, carry):
        at = pl.ds(pl.multiple_of(m * step, step), step)
        hi_ref[at, :], lo_ref[at, :] = halves(x_ref[at, :])
        return carry

    lax.fori_loop(0, x_ref.shape[0] // step, body, 0)


def split_kernel(rows, left_ref, right_ref, mats_ref, order_ref):
    width = left_ref.shape[0]
    half = width // 2
    mine = lax.axis_index("op_2") == 0
    for q in range(width // (2 * rows)):
        a = left_ref[2 * q * rows : (2 * q + 1) * rows, :]
        b = left_ref[(2 * q + 1) * rows : (2 * q + 2) * rows, :]
        order_ref[q * rows : (q + 1) * rows, :] = jnp.where(mine, b, a)
        order_ref[half + q * rows : half + (q + 1) * rows, :] = jnp.where(mine, a, b)
    split_rows(order_ref, mats_ref.at[0], mats_ref.at[1])
    split_rows(right_ref, mats_ref.at[2], mats_ref.at[3])


def left_product(mats_ref, ih_ref, il_ref, out_ref, first, per_row):
    step = 160
    for m in range(out_ref.shape[0] // per_row // step):
        at = pl.ds(first + m * step, step)
        y = dot3(mats_ref[0, at, :], mats_ref[1, at, :], ih_ref[...], il_ref[...])
        for k in range(per_row):
            out_ref[pl.ds(m * step * per_row + k, step, stride=per_row), :] = y[:, k * LANES : (k + 1) * LANES]


def inner_kernel(per_row, x_ref, mats_ref, ih_ref, il_ref, out_ref):
    width = mats_ref.shape[1]
    step = 160
    for m in range(width // step):
        x = jnp.concatenate(
            [x_ref[pl.ds(m * step * per_row + k, step, stride=per_row), :] for k in range(per_row)], axis=1
        )
        x_hi, x_lo = halves(x)
        at = pl.ds(m * step, step)
        ih_ref[at, :], il_ref[at, :] = halves(dot3(x_hi, x_lo, mats_ref[2], mats_ref[3]))
    left_product(mats_ref, ih_ref, il_ref, out_ref, 0, per_row)


def own_kernel(per_row, mats_ref, ih_ref, il_ref, out_ref):
    left_product(mats_ref, ih_ref, il_ref, out_ref, mats_ref.shape[1] // 2, per_row)


def masked_sum(part_ref, slots_ref, lines, per_row):
    parts = part_ref.shape[0] // lines
    w = part_ref[0:lines, :]
    for q in range(1, parts):
        w = w + part_ref[q * lines : (q + 1) * lines, :]
    keep = row_mask(slots_ref[slots_ref.shape[0] - 1], lines, per_row, op_position() * (lines // per_row))
    return jnp.where(keep, w, 0.0)


def share_kernel(lines, per_row, nsec, slots_ref, part_ref, w_ref, out_ref):
    w = masked_sum(part_ref, slots_ref, lines, per_row)
    w_ref[...] = w
    for y in range(nsec):
        out_ref[y * lines : (y + 1) * lines, :] = w


def first_sums_kernel(v8_ref, w8_ref, out_ref):
    v = v8_ref[...]
    out_ref[...] = jnp.broadcast_to(lane_row([total(v * v), total(v * w8_ref[...])]), out_ref.shape)


def update_kernel(lines, pad, nsec, count, slots_ref, sums_ref, v8_ref, d8_ref, w8_ref, out_ref, t_ref, scal_ref, t8_ref):
    sums = jnp.sum(sums_ref[...], axis=0, keepdims=True) / count
    norm, product = sums[:, 0:1], sums[:, 1:2]
    scale = 1.0 / jnp.sqrt(norm + EPS)
    rayleigh = product / (norm + EPS)
    me = lax.axis_index("sec")
    for y in range(nsec):
        k = lax.rem(me + nsec - y, nsec)
        d = d8_ref[pl.ds(pl.multiple_of(k * pad, 8), lines), :]
        at = slice(y * lines, (y + 1) * lines)
        t8_ref[y * pad : y * pad + lines, :] = (scale * w8_ref[at, :] - rayleigh * (scale * v8_ref[at, :])) / d
    t_ref[...] = t8_ref[pl.ds(pl.multiple_of(me * pad, 8), lines), :]
    scal_ref[...] = jnp.broadcast_to(lane_row([norm, product]), scal_ref.shape)
    for t in range(out_ref.shape[0] // lines):
        out_ref[t * lines : (t + 1) * lines, :] = pick(t8_ref, slots_ref, t, lines, pad)


def last_sums_kernel(lines, per_row, pad, slots_ref, part_ref, scal_ref, v_ref, w_ref, t_ref, d_ref, out_ref, keep_ref):
    h = masked_sum(part_ref, slots_ref, lines, per_row)
    scale = 1.0 / jnp.sqrt(scal_ref[0:1, 0:1] + EPS)
    v0 = scale * v_ref[...]
    w0 = scale * w_ref[...]
    t = t_ref[...]
    for i, x in enumerate((v0, w0, t, h, d_ref[0:lines, :])):
        keep_ref[i * pad : i * pad + lines, :] = x
    keep_ref[5 * pad : 5 * pad + 8, :] = scal_ref[...]
    sums = [total(v0 * t), total(t * t), total(t * w0), total(t * h), total(v0 * h)]
    out_ref[...] = jnp.broadcast_to(lane_row(sums), out_ref.shape)


def relay_kernel(in_ref, out_ref):
    out_ref[...] = jnp.broadcast_to(jnp.sum(in_ref[...], axis=0, keepdims=True), out_ref.shape)


def final_kernel(count, per_row, lines, pad, sums_ref, keep_ref, new_ref, corr_ref, new_lines, corr_lines):
    norm, product = keep_ref[5 * pad : 5 * pad + 1, 0:1], keep_ref[5 * pad : 5 * pad + 1, 1:2]
    v0, w0, t, h, d = (keep_ref[i * pad : i * pad + lines, :] for i in range(5))
    sums = jnp.sum(sums_ref[...], axis=0, keepdims=True) / count
    along, tt, tw, th, vh = (sums[:, i : i + 1] for i in range(5))
    rayleigh = product / (norm + EPS)
    vv = norm / (norm + EPS)
    tail = tt - 2.0 * along * along + along * along * vv
    inv = 1.0 / jnp.sqrt(tail + EPS)
    corner = inv * inv * (th - along * (tw + vh) + along * along * rayleigh)
    couple = inv * (tw - along * rayleigh)
    y = 2.0 * couple
    x = rayleigh - corner
    big = jnp.maximum(jnp.abs(x), jnp.abs(y))
    none = big == 0.0
    big = jnp.where(none, 1.0, big)
    xs = jnp.where(none, 1.0, x / big)
    ys = y / big
    hyp = jnp.sqrt(xs * xs + ys * ys)
    major = jnp.sqrt((hyp + jnp.abs(xs)) / (2.0 * hyp))
    minor = jnp.abs(ys) / (2.0 * hyp * major)
    ahead = xs > 0.0
    cosine = jnp.where(ahead, major, minor)
    sine = jnp.where(ys < 0.0, -1.0, 1.0) * jnp.where(ahead, minor, major)
    v1 = inv * (t - along * v0)
    w1 = inv * (h - along * w0)
    new = sine * v0 - cosine * v1
    applied = sine * w0 - cosine * w1
    lam = sine * sine * rayleigh + cosine * cosine * corner - 2.0 * sine * cosine * couple
    new_lines[...] = new
    corr_lines[...] = (applied - lam * new) / d
    rows = new_ref.shape[0]
    for k in range(per_row):
        at, part = pl.ds(k, rows, stride=per_row), slice(k * LANES, (k + 1) * LANES)
        new_ref[:, 0, part] = new_lines[at, :]
        corr_ref[:, 0, part] = corr_lines[at, :]


def f32(*shape):
    return jax.ShapeDtypeStruct(shape, jnp.float32)


def bf16(*shape):
    return jax.ShapeDtypeStruct(shape, jnp.bfloat16)


def call(kernel, out, smem, vmem, scratch=(), anywhere=(), out_anywhere=0, out_smem=0, limit=32 * 1024 * 1024):
    outs = out if isinstance(out, tuple) else (out,)
    specs = [ANY] * out_anywhere + [VMEM] * (len(outs) - out_anywhere - out_smem) + [SMEM] * out_smem
    return pl.pallas_call(
        kernel,
        out_shape=out,
        in_specs=[SMEM] * len(smem) + [ANY] * len(anywhere) + [VMEM] * len(vmem),
        out_specs=tuple(specs) if isinstance(out, tuple) else specs[0],
        scratch_shapes=scratch,
        compiler_params=pltpu.CompilerParams(vmem_limit_bytes=limit),
    )(*smem, *anywhere, *vmem)


def exchange(x, axis, parts):
    lines = x.shape[0] // parts
    y = lax.all_to_all(x.reshape(parts, lines, 1, LANES), axis, 0, 0, tiled=True)
    return y.reshape(x.shape)


def per_device(psi, left_env, right_env, denominators, source_sector, owner, orders):
    rows = psi.shape[0]
    width = psi.shape[2]
    per_row = width // LANES
    lines = rows * per_row
    pad = up8(lines)
    nop = lax.axis_size(OP)
    nchip = lax.axis_size(CHIP)
    nsec = lax.axis_size("sec")
    count = float(width * nsec * width)
    left = left_env.reshape(width, width)
    right = right_env.reshape(width, width)
    source = source_sector.T
    part = functools.partial
    swap = [(0, 1), (1, 0)]

    v, v_out, d_out, slots = call(
        part(prep_kernel, per_row, nsec, pad),
        (
            f32(lines, LANES),
            f32(nsec * lines, LANES),
            f32(pad, LANES),
            jax.ShapeDtypeStruct((nop + 1,), jnp.int32),
        ),
        (),
        (),
        limit=None,
        out_smem=1,
        anywhere=(owner, orders, source, psi, denominators),
        scratch=[
            pltpu.SMEM((nsec,), jnp.int32),
            pltpu.SMEM((nsec,), jnp.int32),
            pltpu.SMEM(source.shape, jnp.int32),
            pltpu.VMEM(psi.shape, jnp.float32),
            pltpu.VMEM(psi.shape, jnp.float32),
            pltpu.SemaphoreType.DMA((5,)),
        ],
    )
    v8 = exchange(v_out, "sec", nsec)
    square = bf16(width, width)
    half = f32(width * per_row // 2, LANES)
    mats = call(
        part(split_kernel, rows),
        bf16(4, width, width),
        (),
        (left, right),
        scratch=[pltpu.VMEM((width, width), jnp.float32)],
    )

    table = pltpu.VMEM((nsec * pad, LANES), jnp.float32)
    whole = [pltpu.VMEM((nop * lines, LANES), jnp.float32), pltpu.SemaphoreType.DMA((PIECES,))]

    def products(x):
        ih, il, other = call(part(inner_kernel, per_row), (square, square, half), (), (x, mats))
        came = lax.ppermute(other, "op_2", swap)
        own = call(part(own_kernel, per_row), half, (), (mats, ih, il))
        return exchange(own + came, CHIP, nchip)

    chosen = call(
        part(select_kernel, lines, pad, nsec),
        f32(nop * lines, LANES),
        (slots,),
        (v8,),
        scratch=[table, *whole],
        out_anywhere=1,
    )
    chosen, d8 = lax.optimization_barrier((chosen, d_out))
    chosen = exchange(chosen, OP, nop)
    reach = 1
    while reach < nsec:
        came = lax.ppermute(d8, "sec", [(i, (i + reach) % nsec) for i in range(nsec)])
        d8 = jnp.concatenate([d8, came], axis=0)
        reach *= 2
    chosen, d8 = lax.optimization_barrier((chosen, d8))
    parts = products(chosen)
    w, w_out = call(
        part(share_kernel, lines, per_row, nsec),
        (f32(lines, LANES), f32(nsec * lines, LANES)),
        (slots,),
        (parts,),
    )
    w8 = exchange(w_out, "sec", nsec)
    sums = call(first_sums_kernel, f32(nop, LANES), (), (v8, w8))
    sums = exchange(sums, OP, nop)
    chosen, t, scal = call(
        part(update_kernel, lines, pad, nsec, count),
        (f32(nop * lines, LANES), f32(lines, LANES), f32(8, LANES)),
        (slots,),
        (sums, v8, d8, w8),
        scratch=[table],
    )
    parts = products(exchange(chosen, OP, nop))
    near = ("op_0", "op_2", "sec")
    sums, keep = call(
        part(last_sums_kernel, lines, per_row, pad),
        (f32(lax.axis_size(near), LANES), f32(5 * pad + 8, LANES)),
        (slots,),
        (parts, scal, v, w, t, d_out),
    )
    sums = exchange(sums, near, lax.axis_size(near))
    far = lax.axis_size("op_1")
    sums = call(relay_kernel, f32(far, LANES), (), (sums,))
    return call(
        part(final_kernel, count, per_row, lines, pad),
        (f32(*psi.shape), f32(*psi.shape)),
        (),
        (exchange(sums, "op_1", far), keep),
        scratch=[pltpu.VMEM((lines, LANES), jnp.float32)] * 2,
    )


def solution(mesh):
    sec = mesh.shape["sec"]
    torus = Mesh(mesh.devices.reshape(4, 8, 2, sec), (*OP, "sec"))
    specs = (
        P(OP, "sec", None),
        P(OP, "sec", None, None),
        P(OP, "sec", None, None),
        P(OP, "sec", None),
        P(),
        P(),
        P(),
    )
    outs = (P(OP, "sec", None), P(OP, "sec", None))
    return jax.shard_map(per_device, mesh=torus, in_specs=specs, out_specs=outs, check_vma=False)
```

```python
import functools

import jax
import jax.numpy as jnp
from jax import lax
from jax.experimental import pallas as pl
from jax.experimental.pallas import tpu as pltpu
from jax.sharding import Mesh
from jax.sharding import PartitionSpec as P

CHIP = ("op_0", "op_1")
OP = ("op_0", "op_1", "op_2")
EPS = 1e-06
LANES = 128
VMEM = pl.BlockSpec(memory_space=pltpu.VMEM)
SMEM = pl.BlockSpec(memory_space=pltpu.SMEM)
ANY = pl.BlockSpec(memory_space=pl.ANY)


def up8(n):
    return -(-n // 8) * 8


def op_position():
    sizes = [lax.axis_size(a) for a in OP]
    return (lax.axis_index("op_0") * sizes[1] + lax.axis_index("op_1")) * sizes[2] + lax.axis_index("op_2")


def sector_at(owner_ref, slot, nsec):
    found = jnp.int32(0)
    for s in range(nsec):
        found = found + jnp.where(owner_ref[s] == slot, s, 0)
    return found


def row_mask(order, lines, per_row, first_row):
    line = lax.broadcasted_iota(jnp.int32, (lines, LANES), 0)
    lane = lax.broadcasted_iota(jnp.int32, (lines, LANES), 1)
    row = line // per_row
    col = (line - row * per_row) * LANES + lane
    return (first_row + row < order) & (col < order)


def total(x):
    return jnp.sum(jnp.sum(x, axis=0, keepdims=True), axis=1, keepdims=True)


def lane_row(values):
    lane = lax.broadcasted_iota(jnp.int32, (1, LANES), 1)
    out = jnp.zeros((1, LANES), jnp.float32)
    for i, v in enumerate(values):
        out = jnp.where(lane == i, v, out)
    return out


def prep_kernel(per_row, nsec, pad, owner_in, orders_in, source_in, psi_in, den_in, v_ref, v_out_ref, d_out_ref, slots_ref, owner_ref, orders_ref, source_ref, psi_ref, den_ref, sems):
    ends = ((owner_in, owner_ref), (orders_in, orders_ref), (source_in, source_ref), (psi_in, psi_ref), (den_in, den_ref))
    copies = [pltpu.make_async_copy(src, dst, sems.at[i]) for i, (src, dst) in enumerate(ends)]
    for c in copies:
        c.start()
    rows, width = psi_ref.shape[0], psi_ref.shape[2]
    lines = rows * per_row
    if pad > lines:
        d_out_ref[lines:pad, :] = jnp.ones((pad - lines, LANES), jnp.float32)
    row = lax.broadcasted_iota(jnp.int32, (rows, width), 0) + op_position() * rows
    col = lax.broadcasted_iota(jnp.int32, (rows, width), 1)
    for c in copies:
        c.wait()
    sector = sector_at(owner_ref, lax.axis_index("sec"), nsec)
    order = orders_ref[sector]
    for t in range(slots_ref.shape[0] - 1):
        slots_ref[t] = owner_ref[source_ref[sector, t]]
    slots_ref[slots_ref.shape[0] - 1] = order
    v = jnp.where((row < order) & (col < order), psi_ref[:, 0, :], 0.0)
    d = den_ref[:, 0, :]
    for k in range(per_row):
        part = slice(k * LANES, (k + 1) * LANES)
        at = pl.ds(k, rows, stride=per_row)
        v_ref[at, :] = v[:, part]
        d_out_ref[at, :] = d[:, part]
        for y in range(nsec):
            v_out_ref[pl.ds(y * lines + k, rows, stride=per_row), :] = v[:, part]


PIECES = 4


def pick(table_ref, slots_ref, t, lines, pitch):
    return table_ref[pl.ds(pl.multiple_of(slots_ref[t] * pitch, 8), lines), :]


def select_kernel(lines, pad, nsec, slots_ref, v8_ref, out_ref, table_ref, buf_ref, sems):
    for y in range(nsec):
        table_ref[y * pad : y * pad + lines, :] = v8_ref[y * lines : (y + 1) * lines, :]
    terms = out_ref.shape[0] // lines
    copies = []
    for c in range(PIECES):
        for t in range(c * terms // PIECES, (c + 1) * terms // PIECES):
            buf_ref[t * lines : (t + 1) * lines, :] = pick(table_ref, slots_ref, t, lines, pad)
        at = pl.ds(c * (terms * lines // PIECES), terms * lines // PIECES)
        copies.append(pltpu.make_async_copy(buf_ref.at[at], out_ref.at[at], sems.at[c]))
        copies[-1].start()
    for c in copies:
        c.wait()


def halves(x):
    hi = x.astype(jnp.bfloat16)
    return hi, (x - hi.astype(jnp.float32)).astype(jnp.bfloat16)


def dot3(a_hi, a_lo, b_hi, b_lo):
    dot = functools.partial(jnp.dot, preferred_element_type=jnp.float32)
    return dot(a_hi, b_hi) + (dot(a_hi, b_lo) + dot(a_lo, b_hi))


def split_rows(x_ref, hi_ref, lo_ref):
    step = 160

    def body(m, carry):
        at = pl.ds(pl.multiple_of(m * step, step), step)
        hi_ref[at, :], lo_ref[at, :] = halves(x_ref[at, :])
        return carry

    lax.fori_loop(0, x_ref.shape[0] // step, body, 0)


def split_kernel(rows, left_ref, right_ref, mats_ref, order_ref):
    width = left_ref.shape[0]
    half = width // 2
    mine = lax.axis_index("op_2") == 0
    for q in range(width // (2 * rows)):
        a = left_ref[2 * q * rows : (2 * q + 1) * rows, :]
        b = left_ref[(2 * q + 1) * rows : (2 * q + 2) * rows, :]
        order_ref[q * rows : (q + 1) * rows, :] = jnp.where(mine, b, a)
        order_ref[half + q * rows : half + (q + 1) * rows, :] = jnp.where(mine, a, b)
    split_rows(order_ref, mats_ref.at[0], mats_ref.at[1])
    split_rows(right_ref, mats_ref.at[2], mats_ref.at[3])


def left_product(mats_ref, ih_ref, il_ref, out_ref, first, per_row):
    step = 320
    weights = jnp.concatenate([ih_ref[...], il_ref[...], ih_ref[...]], axis=0)
    for m in range(out_ref.shape[0] // per_row // step):
        at = pl.ds(first + m * step, step)
        hi = mats_ref[0, at, :]
        y = jnp.dot(jnp.concatenate([hi, hi, mats_ref[1, at, :]], axis=1), weights, preferred_element_type=jnp.float32)
        for k in range(per_row):
            out_ref[pl.ds(m * step * per_row + k, step, stride=per_row), :] = y[:, k * LANES : (k + 1) * LANES]


def inner_kernel(per_row, x_ref, mats_ref, ih_ref, il_ref, out_ref):
    width = mats_ref.shape[1]
    step = 640
    weights = jnp.concatenate([mats_ref[2], mats_ref[3], mats_ref[2]], axis=0)
    for m in range(width // step):
        x = jnp.concatenate(
            [x_ref[pl.ds(m * step * per_row + k, step, stride=per_row), :] for k in range(per_row)], axis=1
        )
        x_hi, x_lo = halves(x)
        at = pl.ds(m * step, step)
        y = jnp.dot(jnp.concatenate([x_hi, x_hi, x_lo], axis=1), weights, preferred_element_type=jnp.float32)
        ih_ref[at, :], il_ref[at, :] = halves(y)
    left_product(mats_ref, ih_ref, il_ref, out_ref, 0, per_row)


def own_kernel(per_row, mats_ref, ih_ref, il_ref, out_ref):
    left_product(mats_ref, ih_ref, il_ref, out_ref, mats_ref.shape[1] // 2, per_row)


def masked_sum(part_ref, slots_ref, lines, per_row):
    parts = part_ref.shape[0] // lines
    w = part_ref[0:lines, :]
    for q in range(1, parts):
        w = w + part_ref[q * lines : (q + 1) * lines, :]
    keep = row_mask(slots_ref[slots_ref.shape[0] - 1], lines, per_row, op_position() * (lines // per_row))
    return jnp.where(keep, w, 0.0)


def share_kernel(lines, per_row, nsec, slots_ref, part_ref, w_ref, out_ref):
    w = masked_sum(part_ref, slots_ref, lines, per_row)
    w_ref[...] = w
    for y in range(nsec):
        out_ref[y * lines : (y + 1) * lines, :] = w


def first_sums_kernel(v8_ref, w8_ref, out_ref):
    v = v8_ref[...]
    out_ref[...] = jnp.broadcast_to(lane_row([total(v * v), total(v * w8_ref[...])]), out_ref.shape)


def update_kernel(lines, pad, nsec, count, slots_ref, sums_ref, v8_ref, d8_ref, w8_ref, out_ref, t_ref, scal_ref, t8_ref):
    sums = jnp.sum(sums_ref[...], axis=0, keepdims=True) / count
    norm, product = sums[:, 0:1], sums[:, 1:2]
    scale = 1.0 / jnp.sqrt(norm + EPS)
    rayleigh = product / (norm + EPS)
    me = lax.axis_index("sec")
    for y in range(nsec):
        k = lax.rem(me + nsec - y, nsec)
        d = d8_ref[pl.ds(pl.multiple_of(k * pad, 8), lines), :]
        at = slice(y * lines, (y + 1) * lines)
        t8_ref[y * pad : y * pad + lines, :] = (scale * w8_ref[at, :] - rayleigh * (scale * v8_ref[at, :])) / d
    t_ref[...] = t8_ref[pl.ds(pl.multiple_of(me * pad, 8), lines), :]
    scal_ref[...] = jnp.broadcast_to(lane_row([norm, product]), scal_ref.shape)
    for t in range(out_ref.shape[0] // lines):
        out_ref[t * lines : (t + 1) * lines, :] = pick(t8_ref, slots_ref, t, lines, pad)


def last_sums_kernel(lines, per_row, pad, slots_ref, part_ref, scal_ref, v_ref, w_ref, t_ref, d_ref, out_ref, keep_ref):
    h = masked_sum(part_ref, slots_ref, lines, per_row)
    scale = 1.0 / jnp.sqrt(scal_ref[0:1, 0:1] + EPS)
    v0 = scale * v_ref[...]
    w0 = scale * w_ref[...]
    t = t_ref[...]
    for i, x in enumerate((v0, w0, t, h, d_ref[0:lines, :])):
        keep_ref[i * pad : i * pad + lines, :] = x
    keep_ref[5 * pad : 5 * pad + 8, :] = scal_ref[...]
    sums = [total(v0 * t), total(t * t), total(t * w0), total(t * h), total(v0 * h)]
    out_ref[...] = jnp.broadcast_to(lane_row(sums), out_ref.shape)


def relay_kernel(in_ref, out_ref):
    out_ref[...] = jnp.broadcast_to(jnp.sum(in_ref[...], axis=0, keepdims=True), out_ref.shape)


def final_kernel(count, per_row, lines, pad, sums_ref, keep_ref, new_ref, corr_ref, new_lines, corr_lines):
    norm, product = keep_ref[5 * pad : 5 * pad + 1, 0:1], keep_ref[5 * pad : 5 * pad + 1, 1:2]
    v0, w0, t, h, d = (keep_ref[i * pad : i * pad + lines, :] for i in range(5))
    sums = jnp.sum(sums_ref[...], axis=0, keepdims=True) / count
    along, tt, tw, th, vh = (sums[:, i : i + 1] for i in range(5))
    rayleigh = product / (norm + EPS)
    vv = norm / (norm + EPS)
    tail = tt - 2.0 * along * along + along * along * vv
    inv = 1.0 / jnp.sqrt(tail + EPS)
    corner = inv * inv * (th - along * (tw + vh) + along * along * rayleigh)
    couple = inv * (tw - along * rayleigh)
    y = 2.0 * couple
    x = rayleigh - corner
    big = jnp.maximum(jnp.abs(x), jnp.abs(y))
    none = big == 0.0
    big = jnp.where(none, 1.0, big)
    xs = jnp.where(none, 1.0, x / big)
    ys = y / big
    hyp = jnp.sqrt(xs * xs + ys * ys)
    major = jnp.sqrt((hyp + jnp.abs(xs)) / (2.0 * hyp))
    minor = jnp.abs(ys) / (2.0 * hyp * major)
    ahead = xs > 0.0
    cosine = jnp.where(ahead, major, minor)
    sine = jnp.where(ys < 0.0, -1.0, 1.0) * jnp.where(ahead, minor, major)
    v1 = inv * (t - along * v0)
    w1 = inv * (h - along * w0)
    new = sine * v0 - cosine * v1
    applied = sine * w0 - cosine * w1
    lam = sine * sine * rayleigh + cosine * cosine * corner - 2.0 * sine * cosine * couple
    new_lines[...] = new
    corr_lines[...] = (applied - lam * new) / d
    rows = new_ref.shape[0]
    for k in range(per_row):
        at, part = pl.ds(k, rows, stride=per_row), slice(k * LANES, (k + 1) * LANES)
        new_ref[:, 0, part] = new_lines[at, :]
        corr_ref[:, 0, part] = corr_lines[at, :]


def f32(*shape):
    return jax.ShapeDtypeStruct(shape, jnp.float32)


def bf16(*shape):
    return jax.ShapeDtypeStruct(shape, jnp.bfloat16)


def call(kernel, out, smem, vmem, scratch=(), anywhere=(), out_anywhere=0, out_smem=0, limit=32 * 1024 * 1024):
    outs = out if isinstance(out, tuple) else (out,)
    specs = [ANY] * out_anywhere + [VMEM] * (len(outs) - out_anywhere - out_smem) + [SMEM] * out_smem
    return pl.pallas_call(
        kernel,
        out_shape=out,
        in_specs=[SMEM] * len(smem) + [ANY] * len(anywhere) + [VMEM] * len(vmem),
        out_specs=tuple(specs) if isinstance(out, tuple) else specs[0],
        scratch_shapes=scratch,
        compiler_params=pltpu.CompilerParams(vmem_limit_bytes=limit),
    )(*smem, *anywhere, *vmem)


def exchange(x, axis, parts):
    lines = x.shape[0] // parts
    y = lax.all_to_all(x.reshape(parts, lines, 1, LANES), axis, 0, 0, tiled=True)
    return y.reshape(x.shape)


def per_device(psi, left_env, right_env, denominators, source_sector, owner, orders):
    rows = psi.shape[0]
    width = psi.shape[2]
    per_row = width // LANES
    lines = rows * per_row
    pad = up8(lines)
    nop = lax.axis_size(OP)
    nchip = lax.axis_size(CHIP)
    nsec = lax.axis_size("sec")
    count = float(width * nsec * width)
    left = left_env.reshape(width, width)
    right = right_env.reshape(width, width)
    source = source_sector.T
    part = functools.partial
    swap = [(0, 1), (1, 0)]

    v, v_out, d_out, slots = call(
        part(prep_kernel, per_row, nsec, pad),
        (
            f32(lines, LANES),
            f32(nsec * lines, LANES),
            f32(pad, LANES),
            jax.ShapeDtypeStruct((nop + 1,), jnp.int32),
        ),
        (),
        (),
        limit=None,
        out_smem=1,
        anywhere=(owner, orders, source, psi, denominators),
        scratch=[
            pltpu.SMEM((nsec,), jnp.int32),
            pltpu.SMEM((nsec,), jnp.int32),
            pltpu.SMEM(source.shape, jnp.int32),
            pltpu.VMEM(psi.shape, jnp.float32),
            pltpu.VMEM(psi.shape, jnp.float32),
            pltpu.SemaphoreType.DMA((5,)),
        ],
    )
    v8 = exchange(v_out, "sec", nsec)
    square = bf16(width, width)
    half = f32(width * per_row // 2, LANES)
    mats = call(
        part(split_kernel, rows),
        bf16(4, width, width),
        (),
        (left, right),
        scratch=[pltpu.VMEM((width, width), jnp.float32)],
    )

    table = pltpu.VMEM((nsec * pad, LANES), jnp.float32)
    whole = [pltpu.VMEM((nop * lines, LANES), jnp.float32), pltpu.SemaphoreType.DMA((PIECES,))]

    def products(x):
        ih, il, other = call(part(inner_kernel, per_row), (square, square, half), (), (x, mats))
        came = lax.ppermute(other, "op_2", swap)
        own = call(part(own_kernel, per_row), half, (), (mats, ih, il))
        return exchange(own + came, CHIP, nchip)

    chosen = call(
        part(select_kernel, lines, pad, nsec),
        f32(nop * lines, LANES),
        (slots,),
        (v8,),
        scratch=[table, *whole],
        out_anywhere=1,
    )
    chosen, d8 = lax.optimization_barrier((chosen, d_out))
    chosen = exchange(chosen, OP, nop)
    reach = 1
    while reach < nsec:
        came = lax.ppermute(d8, "sec", [(i, (i + reach) % nsec) for i in range(nsec)])
        d8 = jnp.concatenate([d8, came], axis=0)
        reach *= 2
    chosen, d8 = lax.optimization_barrier((chosen, d8))
    parts = products(chosen)
    w, w_out = call(
        part(share_kernel, lines, per_row, nsec),
        (f32(lines, LANES), f32(nsec * lines, LANES)),
        (slots,),
        (parts,),
    )
    w8 = exchange(w_out, "sec", nsec)
    sums = call(first_sums_kernel, f32(nop, LANES), (), (v8, w8))
    sums = exchange(sums, OP, nop)
    chosen, t, scal = call(
        part(update_kernel, lines, pad, nsec, count),
        (f32(nop * lines, LANES), f32(lines, LANES), f32(8, LANES)),
        (slots,),
        (sums, v8, d8, w8),
        scratch=[table],
    )
    parts = products(exchange(chosen, OP, nop))
    near = ("op_0", "op_2", "sec")
    sums, keep = call(
        part(last_sums_kernel, lines, per_row, pad),
        (f32(lax.axis_size(near), LANES), f32(5 * pad + 8, LANES)),
        (slots,),
        (parts, scal, v, w, t, d_out),
    )
    sums = exchange(sums, near, lax.axis_size(near))
    far = lax.axis_size("op_1")
    sums = call(relay_kernel, f32(far, LANES), (), (sums,))
    return call(
        part(final_kernel, count, per_row, lines, pad),
        (f32(*psi.shape), f32(*psi.shape)),
        (),
        (exchange(sums, "op_1", far), keep),
        scratch=[pltpu.VMEM((lines, LANES), jnp.float32)] * 2,
    )


def solution(mesh):
    sec = mesh.shape["sec"]
    torus = Mesh(mesh.devices.reshape(4, 8, 2, sec), (*OP, "sec"))
    specs = (
        P(OP, "sec", None),
        P(OP, "sec", None, None),
        P(OP, "sec", None, None),
        P(OP, "sec", None),
        P(),
        P(),
        P(),
    )
    outs = (P(OP, "sec", None), P(OP, "sec", None))
    return jax.shard_map(per_device, mesh=torus, in_specs=specs, out_specs=outs, check_vma=False)
```

```python
import functools

import jax
import jax.numpy as jnp
from jax import lax
from jax.experimental import pallas as pl
from jax.experimental.pallas import tpu as pltpu
from jax.sharding import Mesh
from jax.sharding import PartitionSpec as P

CHIP = ("op_0", "op_1")
OP = ("op_0", "op_1", "op_2")
EPS = 1e-06
LANES = 128
VMEM = pl.BlockSpec(memory_space=pltpu.VMEM)
SMEM = pl.BlockSpec(memory_space=pltpu.SMEM)
ANY = pl.BlockSpec(memory_space=pl.ANY)


def up8(n):
    return -(-n // 8) * 8


def op_position():
    sizes = [lax.axis_size(a) for a in OP]
    return (lax.axis_index("op_0") * sizes[1] + lax.axis_index("op_1")) * sizes[2] + lax.axis_index("op_2")


def sector_at(owner_ref, slot, nsec):
    found = jnp.int32(0)
    for s in range(nsec):
        found = found + jnp.where(owner_ref[s] == slot, s, 0)
    return found


def row_mask(order, lines, per_row, first_row):
    line = lax.broadcasted_iota(jnp.int32, (lines, LANES), 0)
    lane = lax.broadcasted_iota(jnp.int32, (lines, LANES), 1)
    row = line // per_row
    col = (line - row * per_row) * LANES + lane
    return (first_row + row < order) & (col < order)


def total(x):
    return jnp.sum(jnp.sum(x, axis=0, keepdims=True), axis=1, keepdims=True)


def lane_row(values):
    lane = lax.broadcasted_iota(jnp.int32, (1, LANES), 1)
    out = jnp.zeros((1, LANES), jnp.float32)
    for i, v in enumerate(values):
        out = jnp.where(lane == i, v, out)
    return out


def prep_kernel(per_row, nsec, pad, owner_in, orders_in, source_in, psi_in, den_in, v_ref, v_out_ref, d_out_ref, slots_ref, owner_ref, orders_ref, source_ref, psi_ref, den_ref, sems):
    ends = ((owner_in, owner_ref), (orders_in, orders_ref), (source_in, source_ref), (psi_in, psi_ref), (den_in, den_ref))
    copies = [pltpu.make_async_copy(src, dst, sems.at[i]) for i, (src, dst) in enumerate(ends)]
    for c in copies:
        c.start()
    rows, width = psi_ref.shape[0], psi_ref.shape[2]
    lines = rows * per_row
    if pad > lines:
        d_out_ref[lines:pad, :] = jnp.ones((pad - lines, LANES), jnp.float32)
    row = lax.broadcasted_iota(jnp.int32, (rows, width), 0) + op_position() * rows
    col = lax.broadcasted_iota(jnp.int32, (rows, width), 1)
    for c in copies:
        c.wait()
    sector = sector_at(owner_ref, lax.axis_index("sec"), nsec)
    order = orders_ref[sector]
    for t in range(slots_ref.shape[0] - 1):
        slots_ref[t] = owner_ref[source_ref[sector, t]]
    slots_ref[slots_ref.shape[0] - 1] = order
    v = jnp.where((row < order) & (col < order), psi_ref[:, 0, :], 0.0)
    d = den_ref[:, 0, :]
    for k in range(per_row):
        part = slice(k * LANES, (k + 1) * LANES)
        at = pl.ds(k, rows, stride=per_row)
        v_ref[at, :] = v[:, part]
        d_out_ref[at, :] = d[:, part]
        for y in range(nsec):
            v_out_ref[pl.ds(y * lines + k, rows, stride=per_row), :] = v[:, part]


PIECES = 4


def pick(table_ref, slots_ref, t, lines, pitch):
    return table_ref[pl.ds(pl.multiple_of(slots_ref[t] * pitch, 8), lines), :]


def select_kernel(lines, pad, nsec, slots_ref, v8_ref, out_ref, table_ref, buf_ref, sems):
    for y in range(nsec):
        table_ref[y * pad : y * pad + lines, :] = v8_ref[y * lines : (y + 1) * lines, :]
    terms = out_ref.shape[0] // lines
    copies = []
    for c in range(PIECES):
        for t in range(c * terms // PIECES, (c + 1) * terms // PIECES):
            buf_ref[t * lines : (t + 1) * lines, :] = pick(table_ref, slots_ref, t, lines, pad)
        at = pl.ds(c * (terms * lines // PIECES), terms * lines // PIECES)
        copies.append(pltpu.make_async_copy(buf_ref.at[at], out_ref.at[at], sems.at[c]))
        copies[-1].start()
    for c in copies:
        c.wait()


def halves(x):
    hi = x.astype(jnp.bfloat16)
    return hi, (x - hi.astype(jnp.float32)).astype(jnp.bfloat16)


def dot3(a_hi, a_lo, b_hi, b_lo):
    dot = functools.partial(jnp.dot, preferred_element_type=jnp.float32)
    return dot(a_hi, b_hi) + (dot(a_hi, b_lo) + dot(a_lo, b_hi))


def split_rows(x_ref, hi_ref, lo_ref):
    step = 160

    def body(m, carry):
        at = pl.ds(pl.multiple_of(m * step, step), step)
        hi_ref[at, :], lo_ref[at, :] = halves(x_ref[at, :])
        return carry

    lax.fori_loop(0, x_ref.shape[0] // step, body, 0)


def split_kernel(rows, left_ref, right_ref, mats_ref, order_ref):
    width = left_ref.shape[0]
    half = width // 2
    mine = lax.axis_index("op_2") == 0
    for q in range(width // (2 * rows)):
        a = left_ref[2 * q * rows : (2 * q + 1) * rows, :]
        b = left_ref[(2 * q + 1) * rows : (2 * q + 2) * rows, :]
        order_ref[q * rows : (q + 1) * rows, :] = jnp.where(mine, b, a)
        order_ref[half + q * rows : half + (q + 1) * rows, :] = jnp.where(mine, a, b)
    split_rows(order_ref, mats_ref.at[0], mats_ref.at[1])
    split_rows(right_ref, mats_ref.at[2], mats_ref.at[3])


def left_product(mats_ref, ih_ref, il_ref, out_ref, first, per_row):
    step = 320
    weights = jnp.concatenate([ih_ref[...], il_ref[...], ih_ref[...]], axis=0)
    for m in range(out_ref.shape[0] // per_row // step):
        at = pl.ds(first + m * step, step)
        hi = mats_ref[0, at, :]
        y = jnp.dot(jnp.concatenate([hi, hi, mats_ref[1, at, :]], axis=1), weights, preferred_element_type=jnp.float32)
        for k in range(per_row):
            out_ref[pl.ds(m * step * per_row + k, step, stride=per_row), :] = y[:, k * LANES : (k + 1) * LANES]


def inner_kernel(per_row, pieces, x_in, mats_ref, ih_ref, il_ref, out_ref, *scratch):
    width = mats_ref.shape[1]
    step = width // pieces
    x_ref, copies = x_in, []
    if scratch:
        x_ref, sems = scratch
        for m in range(pieces):
            at = pl.ds(m * step * per_row, step * per_row)
            copies.append(pltpu.make_async_copy(x_in.at[at], x_ref.at[at], sems.at[m]))
            copies[-1].start()
    weights = jnp.concatenate([mats_ref[2], mats_ref[3], mats_ref[2]], axis=0)
    for m in range(pieces):
        if copies:
            copies[m].wait()
        x = jnp.concatenate(
            [x_ref[pl.ds(m * step * per_row + k, step, stride=per_row), :] for k in range(per_row)], axis=1
        )
        x_hi, x_lo = halves(x)
        at = pl.ds(m * step, step)
        y = jnp.dot(jnp.concatenate([x_hi, x_hi, x_lo], axis=1), weights, preferred_element_type=jnp.float32)
        ih_ref[at, :], il_ref[at, :] = halves(y)
    left_product(mats_ref, ih_ref, il_ref, out_ref, 0, per_row)


def own_kernel(per_row, mats_ref, ih_ref, il_ref, out_ref):
    left_product(mats_ref, ih_ref, il_ref, out_ref, mats_ref.shape[1] // 2, per_row)


def masked_sum(part_ref, slots_ref, lines, per_row):
    parts = part_ref.shape[0] // lines
    w = part_ref[0:lines, :]
    for q in range(1, parts):
        w = w + part_ref[q * lines : (q + 1) * lines, :]
    keep = row_mask(slots_ref[slots_ref.shape[0] - 1], lines, per_row, op_position() * (lines // per_row))
    return jnp.where(keep, w, 0.0)


def share_kernel(lines, per_row, nsec, slots_ref, part_ref, w_ref, out_ref):
    w = masked_sum(part_ref, slots_ref, lines, per_row)
    w_ref[...] = w
    for y in range(nsec):
        out_ref[y * lines : (y + 1) * lines, :] = w


def first_sums_kernel(v8_ref, w8_ref, out_ref):
    v = v8_ref[...]
    out_ref[...] = jnp.broadcast_to(lane_row([total(v * v), total(v * w8_ref[...])]), out_ref.shape)


def update_kernel(lines, pad, nsec, count, slots_ref, sums_ref, v8_ref, d8_ref, w8_ref, out_ref, t_ref, scal_ref, t8_ref):
    sums = jnp.sum(sums_ref[...], axis=0, keepdims=True) / count
    norm, product = sums[:, 0:1], sums[:, 1:2]
    scale = 1.0 / jnp.sqrt(norm + EPS)
    rayleigh = product / (norm + EPS)
    me = lax.axis_index("sec")
    for y in range(nsec):
        k = lax.rem(me + nsec - y, nsec)
        d = d8_ref[pl.ds(pl.multiple_of(k * pad, 8), lines), :]
        at = slice(y * lines, (y + 1) * lines)
        t8_ref[y * pad : y * pad + lines, :] = (scale * w8_ref[at, :] - rayleigh * (scale * v8_ref[at, :])) / d
    t_ref[...] = t8_ref[pl.ds(pl.multiple_of(me * pad, 8), lines), :]
    scal_ref[...] = jnp.broadcast_to(lane_row([norm, product]), scal_ref.shape)
    for t in range(out_ref.shape[0] // lines):
        out_ref[t * lines : (t + 1) * lines, :] = pick(t8_ref, slots_ref, t, lines, pad)


def last_sums_kernel(lines, per_row, pad, slots_ref, part_ref, scal_ref, v_ref, w_ref, t_ref, d_ref, out_ref, keep_ref):
    h = masked_sum(part_ref, slots_ref, lines, per_row)
    scale = 1.0 / jnp.sqrt(scal_ref[0:1, 0:1] + EPS)
    v0 = scale * v_ref[...]
    w0 = scale * w_ref[...]
    t = t_ref[...]
    for i, x in enumerate((v0, w0, t, h, d_ref[0:lines, :])):
        keep_ref[i * pad : i * pad + lines, :] = x
    keep_ref[5 * pad : 5 * pad + 8, :] = scal_ref[...]
    sums = [total(v0 * t), total(t * t), total(t * w0), total(t * h), total(v0 * h)]
    out_ref[...] = jnp.broadcast_to(lane_row(sums), out_ref.shape)


def relay_kernel(in_ref, out_ref):
    out_ref[...] = jnp.broadcast_to(jnp.sum(in_ref[...], axis=0, keepdims=True), out_ref.shape)


def final_kernel(count, per_row, lines, pad, sums_ref, keep_ref, new_ref, corr_ref, new_lines, corr_lines):
    norm, product = keep_ref[5 * pad : 5 * pad + 1, 0:1], keep_ref[5 * pad : 5 * pad + 1, 1:2]
    v0, w0, t, h, d = (keep_ref[i * pad : i * pad + lines, :] for i in range(5))
    sums = jnp.sum(sums_ref[...], axis=0, keepdims=True) / count
    along, tt, tw, th, vh = (sums[:, i : i + 1] for i in range(5))
    rayleigh = product / (norm + EPS)
    vv = norm / (norm + EPS)
    tail = tt - 2.0 * along * along + along * along * vv
    inv = 1.0 / jnp.sqrt(tail + EPS)
    corner = inv * inv * (th - along * (tw + vh) + along * along * rayleigh)
    couple = inv * (tw - along * rayleigh)
    y = 2.0 * couple
    x = rayleigh - corner
    big = jnp.maximum(jnp.abs(x), jnp.abs(y))
    none = big == 0.0
    big = jnp.where(none, 1.0, big)
    xs = jnp.where(none, 1.0, x / big)
    ys = y / big
    hyp = jnp.sqrt(xs * xs + ys * ys)
    major = jnp.sqrt((hyp + jnp.abs(xs)) / (2.0 * hyp))
    minor = jnp.abs(ys) / (2.0 * hyp * major)
    ahead = xs > 0.0
    cosine = jnp.where(ahead, major, minor)
    sine = jnp.where(ys < 0.0, -1.0, 1.0) * jnp.where(ahead, minor, major)
    v1 = inv * (t - along * v0)
    w1 = inv * (h - along * w0)
    new = sine * v0 - cosine * v1
    applied = sine * w0 - cosine * w1
    lam = sine * sine * rayleigh + cosine * cosine * corner - 2.0 * sine * cosine * couple
    new_lines[...] = new
    corr_lines[...] = (applied - lam * new) / d
    rows = new_ref.shape[0]
    for k in range(per_row):
        at, part = pl.ds(k, rows, stride=per_row), slice(k * LANES, (k + 1) * LANES)
        new_ref[:, 0, part] = new_lines[at, :]
        corr_ref[:, 0, part] = corr_lines[at, :]


def f32(*shape):
    return jax.ShapeDtypeStruct(shape, jnp.float32)


def bf16(*shape):
    return jax.ShapeDtypeStruct(shape, jnp.bfloat16)


def call(kernel, out, smem, vmem, scratch=(), anywhere=(), out_anywhere=0, out_smem=0, limit=32 * 1024 * 1024):
    outs = out if isinstance(out, tuple) else (out,)
    specs = [ANY] * out_anywhere + [VMEM] * (len(outs) - out_anywhere - out_smem) + [SMEM] * out_smem
    return pl.pallas_call(
        kernel,
        out_shape=out,
        in_specs=[SMEM] * len(smem) + [ANY] * len(anywhere) + [VMEM] * len(vmem),
        out_specs=tuple(specs) if isinstance(out, tuple) else specs[0],
        scratch_shapes=scratch,
        compiler_params=pltpu.CompilerParams(vmem_limit_bytes=limit),
    )(*smem, *anywhere, *vmem)


def exchange(x, axis, parts):
    lines = x.shape[0] // parts
    y = lax.all_to_all(x.reshape(parts, lines, 1, LANES), axis, 0, 0, tiled=True)
    return y.reshape(x.shape)


def per_device(psi, left_env, right_env, denominators, source_sector, owner, orders):
    rows = psi.shape[0]
    width = psi.shape[2]
    per_row = width // LANES
    lines = rows * per_row
    pad = up8(lines)
    nop = lax.axis_size(OP)
    nchip = lax.axis_size(CHIP)
    nsec = lax.axis_size("sec")
    count = float(width * nsec * width)
    left = left_env.reshape(width, width)
    right = right_env.reshape(width, width)
    source = source_sector.T
    part = functools.partial
    swap = [(0, 1), (1, 0)]

    v, v_out, d_out, slots = call(
        part(prep_kernel, per_row, nsec, pad),
        (
            f32(lines, LANES),
            f32(nsec * lines, LANES),
            f32(pad, LANES),
            jax.ShapeDtypeStruct((nop + 1,), jnp.int32),
        ),
        (),
        (),
        limit=None,
        out_smem=1,
        anywhere=(owner, orders, source, psi, denominators),
        scratch=[
            pltpu.SMEM((nsec,), jnp.int32),
            pltpu.SMEM((nsec,), jnp.int32),
            pltpu.SMEM(source.shape, jnp.int32),
            pltpu.VMEM(psi.shape, jnp.float32),
            pltpu.VMEM(psi.shape, jnp.float32),
            pltpu.SemaphoreType.DMA((5,)),
        ],
    )
    v8 = exchange(v_out, "sec", nsec)
    square = bf16(width, width)
    half = f32(width * per_row // 2, LANES)
    mats = call(
        part(split_kernel, rows),
        bf16(4, width, width),
        (),
        (left, right),
        scratch=[pltpu.VMEM((width, width), jnp.float32)],
    )

    table = pltpu.VMEM((nsec * pad, LANES), jnp.float32)
    whole = [pltpu.VMEM((nop * lines, LANES), jnp.float32), pltpu.SemaphoreType.DMA((PIECES,))]

    def products(x, streamed):
        if streamed:
            scratch = [whole[0], pltpu.SemaphoreType.DMA((2,))]
            made = call(
                part(inner_kernel, per_row, 2), (square, square, half), (), (mats,), anywhere=(x,), scratch=scratch
            )
        else:
            made = call(part(inner_kernel, per_row, 1), (square, square, half), (), (x, mats))
        ih, il, other = made
        came = lax.ppermute(other, "op_2", swap)
        own = call(part(own_kernel, per_row), half, (), (mats, ih, il))
        return exchange(own + came, CHIP, nchip)

    chosen = call(
        part(select_kernel, lines, pad, nsec),
        f32(nop * lines, LANES),
        (slots,),
        (v8,),
        scratch=[table, *whole],
        out_anywhere=1,
    )
    chosen, d8 = lax.optimization_barrier((chosen, d_out))
    chosen = exchange(chosen, OP, nop)
    reach = 1
    while reach < nsec:
        came = lax.ppermute(d8, "sec", [(i, (i + reach) % nsec) for i in range(nsec)])
        d8 = jnp.concatenate([d8, came], axis=0)
        reach *= 2
    chosen, d8 = lax.optimization_barrier((chosen, d8))
    parts = products(chosen, True)
    w, w_out = call(
        part(share_kernel, lines, per_row, nsec),
        (f32(lines, LANES), f32(nsec * lines, LANES)),
        (slots,),
        (parts,),
    )
    w8 = exchange(w_out, "sec", nsec)
    sums = call(first_sums_kernel, f32(nop, LANES), (), (v8, w8))
    sums = exchange(sums, OP, nop)
    chosen, t, scal = call(
        part(update_kernel, lines, pad, nsec, count),
        (f32(nop * lines, LANES), f32(lines, LANES), f32(8, LANES)),
        (slots,),
        (sums, v8, d8, w8),
        scratch=[table],
    )
    parts = products(exchange(chosen, OP, nop), False)
    near = ("op_0", "op_2")
    sums, keep = call(
        part(last_sums_kernel, lines, per_row, pad),
        (f32(lax.axis_size(near), LANES), f32(5 * pad + 8, LANES)),
        (slots,),
        (parts, scal, v, w, t, d_out),
    )
    sums = exchange(sums, near, lax.axis_size(near))
    far = ("op_1", "sec")
    sums = call(relay_kernel, f32(lax.axis_size(far), LANES), (), (sums,))
    return call(
        part(final_kernel, count, per_row, lines, pad),
        (f32(*psi.shape), f32(*psi.shape)),
        (),
        (exchange(sums, far, lax.axis_size(far)), keep),
        scratch=[pltpu.VMEM((lines, LANES), jnp.float32)] * 2,
    )


def solution(mesh):
    sec = mesh.shape["sec"]
    torus = Mesh(mesh.devices.reshape(4, 8, 2, sec), (*OP, "sec"))
    specs = (
        P(OP, "sec", None),
        P(OP, "sec", None, None),
        P(OP, "sec", None, None),
        P(OP, "sec", None),
        P(),
        P(),
        P(),
    )
    outs = (P(OP, "sec", None), P(OP, "sec", None))
    return jax.shard_map(per_device, mesh=torus, in_specs=specs, out_specs=outs, check_vma=False)
```

```python
import functools

import jax
import jax.numpy as jnp
from jax import lax
from jax.experimental import pallas as pl
from jax.experimental.pallas import tpu as pltpu
from jax.sharding import Mesh
from jax.sharding import PartitionSpec as P

CHIP = ("op_0", "op_1")
OP = ("op_0", "op_1", "op_2")
EPS = 1e-06
LANES = 128
VMEM = pl.BlockSpec(memory_space=pltpu.VMEM)
SMEM = pl.BlockSpec(memory_space=pltpu.SMEM)
ANY = pl.BlockSpec(memory_space=pl.ANY)


def up8(n):
    return -(-n // 8) * 8


def op_position():
    sizes = [lax.axis_size(a) for a in OP]
    return (lax.axis_index("op_0") * sizes[1] + lax.axis_index("op_1")) * sizes[2] + lax.axis_index("op_2")


def sector_at(owner_ref, slot, nsec):
    found = jnp.int32(0)
    for s in range(nsec):
        found = found + jnp.where(owner_ref[s] == slot, s, 0)
    return found


def row_mask(order, lines, per_row, first_row):
    line = lax.broadcasted_iota(jnp.int32, (lines, LANES), 0)
    lane = lax.broadcasted_iota(jnp.int32, (lines, LANES), 1)
    row = line // per_row
    col = (line - row * per_row) * LANES + lane
    return (first_row + row < order) & (col < order)


def total(x):
    return jnp.sum(jnp.sum(x, axis=0, keepdims=True), axis=1, keepdims=True)


def lane_row(values):
    lane = lax.broadcasted_iota(jnp.int32, (1, LANES), 1)
    out = jnp.zeros((1, LANES), jnp.float32)
    for i, v in enumerate(values):
        out = jnp.where(lane == i, v, out)
    return out


def prep_kernel(per_row, nsec, pad, owner_in, orders_in, source_in, psi_in, den_in, v_ref, v_out_ref, d_out_ref, slots_ref, owner_ref, orders_ref, source_ref, psi_ref, den_ref, sems):
    ends = ((owner_in, owner_ref), (orders_in, orders_ref), (source_in, source_ref), (psi_in, psi_ref), (den_in, den_ref))
    copies = [pltpu.make_async_copy(src, dst, sems.at[i]) for i, (src, dst) in enumerate(ends)]
    for c in copies:
        c.start()
    rows, width = psi_ref.shape[0], psi_ref.shape[2]
    lines = rows * per_row
    if pad > lines:
        d_out_ref[lines:pad, :] = jnp.ones((pad - lines, LANES), jnp.float32)
    row = lax.broadcasted_iota(jnp.int32, (rows, width), 0) + op_position() * rows
    col = lax.broadcasted_iota(jnp.int32, (rows, width), 1)
    for c in copies:
        c.wait()
    sector = sector_at(owner_ref, lax.axis_index("sec"), nsec)
    order = orders_ref[sector]
    for t in range(slots_ref.shape[0] - 1):
        slots_ref[t] = owner_ref[source_ref[sector, t]]
    slots_ref[slots_ref.shape[0] - 1] = order
    v = jnp.where((row < order) & (col < order), psi_ref[:, 0, :], 0.0)
    d = den_ref[:, 0, :]
    for k in range(per_row):
        part = slice(k * LANES, (k + 1) * LANES)
        at = pl.ds(k, rows, stride=per_row)
        v_ref[at, :] = v[:, part]
        d_out_ref[at, :] = d[:, part]
        for y in range(nsec):
            v_out_ref[pl.ds(y * lines + k, rows, stride=per_row), :] = v[:, part]


PIECES = 8


def pick(table_ref, slots_ref, t, lines, pitch):
    return table_ref[pl.ds(pl.multiple_of(slots_ref[t] * pitch, 8), lines), :]


def select_kernel(lines, pad, nsec, slots_ref, v8_ref, out_ref, table_ref, buf_ref, sems):
    for y in range(nsec):
        table_ref[y * pad : y * pad + lines, :] = v8_ref[y * lines : (y + 1) * lines, :]
    terms = out_ref.shape[0] // lines
    copies = []
    for c in range(PIECES):
        for t in range(c * terms // PIECES, (c + 1) * terms // PIECES):
            buf_ref[t * lines : (t + 1) * lines, :] = pick(table_ref, slots_ref, t, lines, pad)
        at = pl.ds(c * (terms * lines // PIECES), terms * lines // PIECES)
        copies.append(pltpu.make_async_copy(buf_ref.at[at], out_ref.at[at], sems.at[c]))
        copies[-1].start()
    for c in copies:
        c.wait()


def halves(x):
    hi = x.astype(jnp.bfloat16)
    return hi, (x - hi.astype(jnp.float32)).astype(jnp.bfloat16)


def dot3(a_hi, a_lo, b_hi, b_lo):
    dot = functools.partial(jnp.dot, preferred_element_type=jnp.float32)
    return dot(a_hi, b_hi) + (dot(a_hi, b_lo) + dot(a_lo, b_hi))


def split_rows(x_ref, hi_ref, lo_ref):
    step = 160

    def body(m, carry):
        at = pl.ds(pl.multiple_of(m * step, step), step)
        hi_ref[at, :], lo_ref[at, :] = halves(x_ref[at, :])
        return carry

    lax.fori_loop(0, x_ref.shape[0] // step, body, 0)


def split_kernel(rows, left_ref, right_ref, mats_ref, order_ref):
    width = left_ref.shape[0]
    half = width // 2
    mine = lax.axis_index("op_2") == 0
    for q in range(width // (2 * rows)):
        a = left_ref[2 * q * rows : (2 * q + 1) * rows, :]
        b = left_ref[(2 * q + 1) * rows : (2 * q + 2) * rows, :]
        order_ref[q * rows : (q + 1) * rows, :] = jnp.where(mine, b, a)
        order_ref[half + q * rows : half + (q + 1) * rows, :] = jnp.where(mine, a, b)
    split_rows(order_ref, mats_ref.at[0], mats_ref.at[1])
    split_rows(right_ref, mats_ref.at[2], mats_ref.at[3])


def left_product(mats_ref, ih_ref, il_ref, out_ref, first, per_row):
    step = 320
    weights = jnp.concatenate([ih_ref[...], il_ref[...], ih_ref[...]], axis=0)
    for m in range(out_ref.shape[0] // per_row // step):
        at = pl.ds(first + m * step, step)
        hi = mats_ref[0, at, :]
        y = jnp.dot(jnp.concatenate([hi, hi, mats_ref[1, at, :]], axis=1), weights, preferred_element_type=jnp.float32)
        for k in range(per_row):
            out_ref[pl.ds(m * step * per_row + k, step, stride=per_row), :] = y[:, k * LANES : (k + 1) * LANES]


def inner_kernel(per_row, pieces, x_in, mats_ref, ih_ref, il_ref, out_ref, *scratch):
    width = mats_ref.shape[1]
    step = width // pieces
    x_ref, copies = x_in, []
    if scratch:
        x_ref, sems = scratch
        for m in range(pieces):
            at = pl.ds(m * step * per_row, step * per_row)
            copies.append(pltpu.make_async_copy(x_in.at[at], x_ref.at[at], sems.at[m]))
            copies[-1].start()
    weights = jnp.concatenate([mats_ref[2], mats_ref[3], mats_ref[2]], axis=0)
    for m in range(pieces):
        if copies:
            copies[m].wait()
        x = jnp.concatenate(
            [x_ref[pl.ds(m * step * per_row + k, step, stride=per_row), :] for k in range(per_row)], axis=1
        )
        x_hi, x_lo = halves(x)
        at = pl.ds(m * step, step)
        y = jnp.dot(jnp.concatenate([x_hi, x_hi, x_lo], axis=1), weights, preferred_element_type=jnp.float32)
        ih_ref[at, :], il_ref[at, :] = halves(y)
    left_product(mats_ref, ih_ref, il_ref, out_ref, 0, per_row)


def own_kernel(per_row, mats_ref, ih_ref, il_ref, out_ref):
    left_product(mats_ref, ih_ref, il_ref, out_ref, mats_ref.shape[1] // 2, per_row)


def masked_sum(part_ref, slots_ref, lines, per_row):
    parts = part_ref.shape[0] // lines
    w = part_ref[0:lines, :]
    for q in range(1, parts):
        w = w + part_ref[q * lines : (q + 1) * lines, :]
    keep = row_mask(slots_ref[slots_ref.shape[0] - 1], lines, per_row, op_position() * (lines // per_row))
    return jnp.where(keep, w, 0.0)


def share_kernel(lines, per_row, nsec, slots_ref, part_ref, w_ref, out_ref):
    w = masked_sum(part_ref, slots_ref, lines, per_row)
    w_ref[...] = w
    for y in range(nsec):
        out_ref[y * lines : (y + 1) * lines, :] = w


def first_sums_kernel(v8_ref, w8_ref, out_ref):
    v = v8_ref[...]
    out_ref[...] = jnp.broadcast_to(lane_row([total(v * v), total(v * w8_ref[...])]), out_ref.shape)


def update_kernel(lines, pad, nsec, count, slots_ref, sums_ref, v8_ref, d8_ref, w8_ref, out_ref, t_ref, scal_ref, t8_ref):
    sums = jnp.sum(sums_ref[...], axis=0, keepdims=True) / count
    norm, product = sums[:, 0:1], sums[:, 1:2]
    scale = 1.0 / jnp.sqrt(norm + EPS)
    rayleigh = product / (norm + EPS)
    me = lax.axis_index("sec")
    for y in range(nsec):
        k = lax.rem(me + nsec - y, nsec)
        d = d8_ref[pl.ds(pl.multiple_of(k * pad, 8), lines), :]
        at = slice(y * lines, (y + 1) * lines)
        t8_ref[y * pad : y * pad + lines, :] = (scale * w8_ref[at, :] - rayleigh * (scale * v8_ref[at, :])) / d
    t_ref[...] = t8_ref[pl.ds(pl.multiple_of(me * pad, 8), lines), :]
    scal_ref[...] = jnp.broadcast_to(lane_row([norm, product]), scal_ref.shape)
    for t in range(out_ref.shape[0] // lines):
        out_ref[t * lines : (t + 1) * lines, :] = pick(t8_ref, slots_ref, t, lines, pad)


def last_sums_kernel(lines, per_row, pad, slots_ref, part_ref, scal_ref, v_ref, w_ref, t_ref, d_ref, out_ref, keep_ref):
    h = masked_sum(part_ref, slots_ref, lines, per_row)
    scale = 1.0 / jnp.sqrt(scal_ref[0:1, 0:1] + EPS)
    v0 = scale * v_ref[...]
    w0 = scale * w_ref[...]
    t = t_ref[...]
    for i, x in enumerate((v0, w0, t, h, d_ref[0:lines, :])):
        keep_ref[i * pad : i * pad + lines, :] = x
    keep_ref[5 * pad : 5 * pad + 8, :] = scal_ref[...]
    sums = [total(v0 * t), total(t * t), total(t * w0), total(t * h), total(v0 * h)]
    out_ref[...] = jnp.broadcast_to(lane_row(sums), out_ref.shape)


def relay_kernel(in_ref, out_ref):
    out_ref[...] = jnp.broadcast_to(jnp.sum(in_ref[...], axis=0, keepdims=True), out_ref.shape)


def final_kernel(count, per_row, lines, pad, sums_ref, keep_ref, new_ref, corr_ref, new_lines, corr_lines):
    norm, product = keep_ref[5 * pad : 5 * pad + 1, 0:1], keep_ref[5 * pad : 5 * pad + 1, 1:2]
    v0, w0, t, h, d = (keep_ref[i * pad : i * pad + lines, :] for i in range(5))
    sums = jnp.sum(sums_ref[...], axis=0, keepdims=True) / count
    along, tt, tw, th, vh = (sums[:, i : i + 1] for i in range(5))
    rayleigh = product / (norm + EPS)
    vv = norm / (norm + EPS)
    tail = tt - 2.0 * along * along + along * along * vv
    inv = 1.0 / jnp.sqrt(tail + EPS)
    corner = inv * inv * (th - along * (tw + vh) + along * along * rayleigh)
    couple = inv * (tw - along * rayleigh)
    y = 2.0 * couple
    x = rayleigh - corner
    big = jnp.maximum(jnp.abs(x), jnp.abs(y))
    none = big == 0.0
    big = jnp.where(none, 1.0, big)
    xs = jnp.where(none, 1.0, x / big)
    ys = y / big
    hyp = jnp.sqrt(xs * xs + ys * ys)
    major = jnp.sqrt((hyp + jnp.abs(xs)) / (2.0 * hyp))
    minor = jnp.abs(ys) / (2.0 * hyp * major)
    ahead = xs > 0.0
    cosine = jnp.where(ahead, major, minor)
    sine = jnp.where(ys < 0.0, -1.0, 1.0) * jnp.where(ahead, minor, major)
    v1 = inv * (t - along * v0)
    w1 = inv * (h - along * w0)
    new = sine * v0 - cosine * v1
    applied = sine * w0 - cosine * w1
    lam = sine * sine * rayleigh + cosine * cosine * corner - 2.0 * sine * cosine * couple
    new_lines[...] = new
    corr_lines[...] = (applied - lam * new) / d
    rows = new_ref.shape[0]
    for k in range(per_row):
        at, part = pl.ds(k, rows, stride=per_row), slice(k * LANES, (k + 1) * LANES)
        new_ref[:, 0, part] = new_lines[at, :]
        corr_ref[:, 0, part] = corr_lines[at, :]


def f32(*shape):
    return jax.ShapeDtypeStruct(shape, jnp.float32)


def bf16(*shape):
    return jax.ShapeDtypeStruct(shape, jnp.bfloat16)


def call(kernel, out, smem, vmem, scratch=(), anywhere=(), out_anywhere=0, out_smem=0, limit=32 * 1024 * 1024):
    outs = out if isinstance(out, tuple) else (out,)
    specs = [ANY] * out_anywhere + [VMEM] * (len(outs) - out_anywhere - out_smem) + [SMEM] * out_smem
    return pl.pallas_call(
        kernel,
        out_shape=out,
        in_specs=[SMEM] * len(smem) + [ANY] * len(anywhere) + [VMEM] * len(vmem),
        out_specs=tuple(specs) if isinstance(out, tuple) else specs[0],
        scratch_shapes=scratch,
        compiler_params=pltpu.CompilerParams(vmem_limit_bytes=limit),
    )(*smem, *anywhere, *vmem)


def exchange(x, axis, parts):
    lines = x.shape[0] // parts
    y = lax.all_to_all(x.reshape(parts, lines, 1, LANES), axis, 0, 0, tiled=True)
    return y.reshape(x.shape)


def per_device(psi, left_env, right_env, denominators, source_sector, owner, orders):
    rows = psi.shape[0]
    width = psi.shape[2]
    per_row = width // LANES
    lines = rows * per_row
    pad = up8(lines)
    nop = lax.axis_size(OP)
    nchip = lax.axis_size(CHIP)
    nsec = lax.axis_size("sec")
    count = float(width * nsec * width)
    left = left_env.reshape(width, width)
    right = right_env.reshape(width, width)
    source = source_sector.T
    part = functools.partial
    swap = [(0, 1), (1, 0)]

    v, v_out, d_out, slots = call(
        part(prep_kernel, per_row, nsec, pad),
        (
            f32(lines, LANES),
            f32(nsec * lines, LANES),
            f32(pad, LANES),
            jax.ShapeDtypeStruct((nop + 1,), jnp.int32),
        ),
        (),
        (),
        limit=None,
        out_smem=1,
        anywhere=(owner, orders, source, psi, denominators),
        scratch=[
            pltpu.SMEM((nsec,), jnp.int32),
            pltpu.SMEM((nsec,), jnp.int32),
            pltpu.SMEM(source.shape, jnp.int32),
            pltpu.VMEM(psi.shape, jnp.float32),
            pltpu.VMEM(psi.shape, jnp.float32),
            pltpu.SemaphoreType.DMA((5,)),
        ],
    )
    v8 = exchange(v_out, "sec", nsec)
    square = bf16(width, width)
    half = f32(width * per_row // 2, LANES)
    mats = call(
        part(split_kernel, rows),
        bf16(4, width, width),
        (),
        (left, right),
        scratch=[pltpu.VMEM((width, width), jnp.float32)],
    )

    table = pltpu.VMEM((nsec * pad, LANES), jnp.float32)
    whole = [pltpu.VMEM((nop * lines, LANES), jnp.float32), pltpu.SemaphoreType.DMA((PIECES,))]

    def products(x, streamed):
        if streamed:
            scratch = [whole[0], pltpu.SemaphoreType.DMA((2,))]
            made = call(
                part(inner_kernel, per_row, 2), (square, square, half), (), (mats,), anywhere=(x,), scratch=scratch
            )
        else:
            made = call(part(inner_kernel, per_row, 1), (square, square, half), (), (x, mats))
        ih, il, other = made
        came = lax.ppermute(other, "op_2", swap)
        own = call(part(own_kernel, per_row), half, (), (mats, ih, il))
        return exchange(own + came, CHIP, nchip)

    chosen = call(
        part(select_kernel, lines, pad, nsec),
        f32(nop * lines, LANES),
        (slots,),
        (v8,),
        scratch=[table, *whole],
        out_anywhere=1,
    )
    chosen, d8 = lax.optimization_barrier((chosen, d_out))
    chosen = exchange(chosen, OP, nop)
    reach = 1
    while reach < nsec:
        came = lax.ppermute(d8, "sec", [(i, (i + reach) % nsec) for i in range(nsec)])
        d8 = jnp.concatenate([d8, came], axis=0)
        reach *= 2
    chosen, d8 = lax.optimization_barrier((chosen, d8))
    parts = products(chosen, True)
    w, w_out = call(
        part(share_kernel, lines, per_row, nsec),
        (f32(lines, LANES), f32(nsec * lines, LANES)),
        (slots,),
        (parts,),
    )
    w8 = exchange(w_out, "sec", nsec)
    sums = call(first_sums_kernel, f32(nop, LANES), (), (v8, w8))
    sums = exchange(sums, OP, nop)
    chosen, t, scal = call(
        part(update_kernel, lines, pad, nsec, count),
        (f32(nop * lines, LANES), f32(lines, LANES), f32(8, LANES)),
        (slots,),
        (sums, v8, d8, w8),
        scratch=[table],
    )
    parts = products(exchange(chosen, OP, nop), False)
    near = ("op_0", "op_2", "sec")
    sums, keep = call(
        part(last_sums_kernel, lines, per_row, pad),
        (f32(lax.axis_size(near), LANES), f32(5 * pad + 8, LANES)),
        (slots,),
        (parts, scal, v, w, t, d_out),
    )
    sums = exchange(sums, near, lax.axis_size(near))
    far = ("op_1",)
    sums = call(relay_kernel, f32(lax.axis_size(far), LANES), (), (sums,))
    return call(
        part(final_kernel, count, per_row, lines, pad),
        (f32(*psi.shape), f32(*psi.shape)),
        (),
        (exchange(sums, far, lax.axis_size(far)), keep),
        scratch=[pltpu.VMEM((lines, LANES), jnp.float32)] * 2,
    )


def solution(mesh):
    sec = mesh.shape["sec"]
    torus = Mesh(mesh.devices.reshape(4, 8, 2, sec), (*OP, "sec"))
    specs = (
        P(OP, "sec", None),
        P(OP, "sec", None, None),
        P(OP, "sec", None, None),
        P(OP, "sec", None),
        P(),
        P(),
        P(),
    )
    outs = (P(OP, "sec", None), P(OP, "sec", None))
    return jax.shard_map(per_device, mesh=torus, in_specs=specs, out_specs=outs, check_vma=False)
```
